128 devices in a mesh: dp: 8 (over x_hi, z), mp: 16 (over y, x_lo, core).
Axes of the slice: x: 4 (x_hi: 2, x_lo: 2; x = x_hi * 2 + x_lo), y: 4, z: 4, core: 2. Of those that a mesh axis runs over, the one named last changes fastest.
Arguments:
- tokens: bfloat16 [4096, 3072], P('dp', 'mp'), may hold values from -6 to 6
- w_first: bfloat16 [3072, 12288], P('dp', 'mp'), may hold values from -0.15625 to 0.15625
- w_second: bfloat16 [12288, 3072], P('mp', 'dp'), may hold values from -0.078125 to 0.078125
- cotangent: bfloat16 [4096, 3072], P('dp', 'mp'), may hold values from -1.5 to 1.5
Outputs:
- outputs: bfloat16 [4096, 3072], P('dp', 'mp')
- input_grad: bfloat16 [4096, 3072], P('dp', 'mp')
- first_grad: float32 [3072, 12288], P('dp', 'mp')
- second_grad: float32 [12288, 3072], P('mp', 'dp')
The draws below stay inside these ranges and needn't reach their ends.
All inputs are finite; a program needn't handle non-finite values.
Results may differ from the reference program's by a relative error of at most 0.018.
Values may be sent and summed in bfloat16 or wider, within the bound.
A program may use at most 128 MiB of HBM per device.

```python
import jax
import jax.numpy as jnp
from jax import lax

D = 3072
FF = 12288
TOK_DEV = 512
TOKENS = 4096
N_DP = 8
N_MP = 16


def raised(entries, own_key, source, target, shards_of, factor):
    def block_of(dim):
        return (jnp.arange(entries.shape[dim]) // (entries.shape[dim] // shards_of)).reshape((-1,) + (1,) * (entries.ndim - 1 - dim))

    one_side = jax.random.permutation(own_key, shards_of)[block_of(target)]
    other_side = (block_of(target) + shards_of // 2) % shards_of
    return jnp.where((block_of(source) == one_side) | (block_of(source) == other_side), factor * entries, entries)


def steps_of(rng, extent, shards, least, high):
    def one(dim, parts):
        draws = jax.random.uniform(jax.random.fold_in(jax.random.fold_in(rng, 6), dim), (parts,), jnp.float32, least / len(shards), high / len(shards))
        return jnp.repeat(jnp.exp(draws), extent[dim] // parts).reshape((-1,) + (1,) * (len(extent) - dim - 1))

    factor_of = one(*shards[0])
    for cut in shards[1:]:
        factor_of = factor_of * one(*cut)
    return factor_of


def normal_values(own_key, dims, scale, limit, shards=(), dtype=jnp.bfloat16):
    entries = scale * jax.random.normal(own_key, dims, jnp.float32)
    if shards:
        entries = entries * steps_of(own_key, dims, shards, -0.22, 0.18)
    return jnp.clip(entries, -limit, limit).astype(dtype)


def heavy_noise(rng, shape, scale, most, cuts, heavy, kind=jnp.bfloat16):
    values = scale * jax.random.normal(rng, shape, jnp.float32)
    if cuts:
        values = values * steps_of(rng, shape, cuts, -0.22, 0.18)
    return jnp.clip(raised(values, jax.random.fold_in(rng, 3), *heavy), -most, most).astype(kind)


def setup_inputs(seed: int = 0) -> dict:
    arg_keys = jax.random.split(jax.random.key(seed), 5)
    tokens = normal_values(arg_keys[0], (TOKENS, D), 1.0, 6.0, ((0, 8), (1, 16)))
    w_first = heavy_noise(arg_keys[1], (D, FF), D ** -0.5, 0.15625, ((0, 8), (1, 16)), (1, 0, 16, 2.0))
    w_second = heavy_noise(arg_keys[2], (FF, D), FF ** -0.5, 0.078125, ((0, 16), (1, 8)), (0, 1, 16, 2.0))
    cotangent = normal_values(arg_keys[3], (TOKENS, D), 0.25, 1.5, ((0, 8), (1, 16)))
    return dict(tokens=tokens, w_first=w_first, w_second=w_second, cotangent=cotangent)


inv_root_two = 0.7071067811865476
inv_root_tau = 0.3989422804014327


def gelu_value(value):
    return 0.5 * value * (1.0 + lax.erf(value * inv_root_two))


def gelu_slope(value):
    return 0.5 * (1.0 + lax.erf(value * inv_root_two)) + value * jnp.exp(-0.5 * value * value) * inv_root_tau


def rounded(value):
    return lax.optimization_barrier(value.astype(jnp.bfloat16)).astype(jnp.float32)


def reference(tokens, w_first, w_second, cotangent):
    pre_act = jnp.dot(tokens, w_first, preferred_element_type=jnp.float32)
    activated = gelu_value(pre_act).astype(jnp.bfloat16)
    width = FF // N_MP
    act_blocks = activated.reshape(TOKENS, N_MP, width).transpose(1, 0, 2)
    second_blocks = w_second.reshape(N_MP, width, D)

    def add_output(total, pair):
        left, right = pair
        return total + rounded(jnp.dot(left, right, preferred_element_type=jnp.float32)), None

    summed, _ = lax.scan(add_output, jnp.zeros((TOKENS, D), jnp.float32), (act_blocks, second_blocks))
    outputs = summed.astype(jnp.bfloat16)
    back_pre = lax.dot_general(cotangent, w_second, (((1,), (1,)), ((), ())), preferred_element_type=jnp.float32)
    hidden_grad = (back_pre * gelu_slope(pre_act)).astype(jnp.bfloat16)

    def add_second(total, pair):
        left, right = pair
        return total + rounded(lax.dot_general(left, right, (((0,), (0,)), ((), ())), preferred_element_type=jnp.float32)), None

    second_grad, _ = lax.scan(add_second, jnp.zeros((FF, D), jnp.float32),
                              (activated.reshape(N_DP, TOK_DEV, FF), cotangent.reshape(N_DP, TOK_DEV, D)))
    first_grad, _ = lax.scan(add_second, jnp.zeros((D, FF), jnp.float32),
                             (tokens.reshape(N_DP, TOK_DEV, D), hidden_grad.reshape(N_DP, TOK_DEV, FF)))
    grad_blocks = hidden_grad.reshape(TOKENS, N_MP, width).transpose(1, 0, 2)
    first_blocks = w_first.reshape(D, N_MP, width).transpose(1, 0, 2)

    def add_input(total, pair):
        left, right = pair
        return total + rounded(lax.dot_general(left, right, (((1,), (1,)), ((), ())), preferred_element_type=jnp.float32)), None

    input_sum, _ = lax.scan(add_input, jnp.zeros((TOKENS, D), jnp.float32), (grad_blocks, first_blocks))
    input_grad = input_sum.astype(jnp.bfloat16)
    return outputs, input_grad, first_grad, second_grad
```

```python
import jax
import jax.numpy as jnp
from jax import lax
from jax.experimental import pallas as pl
from jax.experimental.pallas import tpu as pltpu
from jax.sharding import Mesh
from jax.sharding import PartitionSpec as P

AXES = ("xh", "z", "y", "xl", "c")
DP = ("xh", "z")
MP = ("y", "xl", "c")
MESH = pl.DeviceIdType.MESH
F32 = jnp.float32
BF16 = jnp.bfloat16

D = 3072
B = 384
HID = 768
TOK = 512
HALF = 256
RA = 176
RB = HALF - RA
SPLIT_A = (96, 80)
SPLIT_B = (48, 32)
NSEM = 200

inv_root_two = 0.7071067811865476
inv_root_tau = 0.3989422804014327


def dot(a, b):
    return jnp.dot(a, b, preferred_element_type=F32)


def dot_nt(a, b):
    return lax.dot_general(a, b, (((1,), (1,)), ((), ())), preferred_element_type=F32)


def mult(value, of):
    return pl.multiple_of(value, of)


class Links:
    def __init__(self, send, recv):
        self.send, self.recv, self.count, self.open = send, recv, 0, []

    def start(self, src, dst, peer):
        i = self.count
        self.count += 1
        copy = pltpu.make_async_remote_copy(
            src_ref=src,
            dst_ref=dst,
            send_sem=self.send.at[i],
            recv_sem=self.recv.at[i],
            device_id=peer,
            device_id_type=MESH,
        )
        copy.start()
        self.open.append(copy)
        return (i, peer)

    def arrived(self, handle, where):
        i, peer = handle
        pltpu.make_async_remote_copy(
            src_ref=where,
            dst_ref=where,
            send_sem=self.send.at[i],
            recv_sem=self.recv.at[i],
            device_id=peer,
            device_id_type=MESH,
        ).wait_recv()

    def flush(self):
        for copy in self.open:
            copy.wait_send()
        self.open = []


def kernel(
    tok_in, cot_in, w1_in, w2_in,
    out_ref, ing_ref, g1_ref, g2_ref,
    w1, w2, tok, cot, tok_t, act, act_t, slope, hg, oterm, p1, p2,
    rsw1, rsw2, rza1, rza2, rzb1, rzb2,
    ra1, ra2, ra3, ra4, rb1, rb2, rb3, rb4,
    swap_in, swap_out, send, recv,
):
    xh, z, y, xl, c = (lax.axis_index(a) for a in AXES)
    x = xh * 2 + xl
    xp, xm = lax.rem(x + 1, 4), lax.rem(x + 3, 4)
    ph, pll = xp // 2, lax.rem(xp, 2)
    mh, ml = xm // 2, lax.rem(xm, 2)
    yp, ym, y2 = lax.rem(y + 1, 4), lax.rem(y + 3, 4), lax.rem(y + 2, 4)
    zp, zm, z2 = lax.rem(z + 1, 4), lax.rem(z + 3, 4), lax.rem(z + 2, 4)
    oc = 1 - c
    XP, XM = {"xh": ph, "xl": pll}, {"xh": mh, "xl": ml}
    YP, YM, ZP, ZM, OC = {"y": yp}, {"y": ym}, {"z": zp}, {"z": zm}, {"c": oc}
    links = Links(send, recv)
    start, arrived = links.start, links.arrived

    bar = pltpu.get_barrier_semaphore()
    for peer in (XP, XM, YP, YM, ZP, ZM, OC):
        pl.semaphore_signal(bar, inc=1, device_id=peer, device_id_type=MESH)
    pl.semaphore_wait(bar, 7)

    def rows_a(hv, lo=0, n=RA):
        return pl.ds(mult(hv * RA + lo, 16), n)

    def rows_b(hv, lo=0, n=RB):
        return pl.ds(mult(2 * RA + hv * RB + lo, 16), n)

    def cols(yv, lv):
        return pl.ds(mult((yv * 2 + lv) * B, 128), B)

    def line(yv):
        return pl.ds(mult(yv * 2 * B, 128), 2 * B)

    def loc1(ref, hv, zv, cv):
        return ref.at[pl.ds(mult((hv * 4 + zv) * B, 128), B), pl.ds(mult(cv * B, 128), B)]

    def loc2(ref, hv, zv, cv):
        return ref.at[pl.ds(mult(cv * B, 128), B), pl.ds(mult((hv * 4 + zv) * B, 128), B)]

    class Weights:
        def __init__(self, shard, ref, loc, half):
            self.ref, self.loc = ref, loc
            self.at = lambda hv, zv: loc(ref, hv, zv, c)
            self.other = lambda hv, zv: loc(ref, hv, zv, oc)
            self.swaps = []
            self.sent = (
                start(half(shard, ph), self.at(xh, z), XP),
                start(half(shard, mh), self.at(xh, z), XM),
            )

        def swap(self, hv, zv):
            block = self.at(hv, zv)
            self.swaps.append((start(block, block, OC), hv, zv))

        def along_z(self):
            left, right = self.at(mh, z), self.at(ph, z)
            arrived(self.sent[0], left)
            lp, lm = start(left, left, ZP), start(left, left, ZM)
            arrived(self.sent[1], right)
            rp, rm = start(right, right, ZP), start(right, right, ZM)
            self.z1 = lp, lm, rp, rm
            self.swap(mh, z)
            self.swap(ph, z)

        def forward_z(self):
            lp, lm, rp, rm = self.z1
            block = self.at(mh, zm)
            arrived(lp, block)
            f1 = start(block, block, ZP)
            block = self.at(ph, zp)
            arrived(rm, block)
            f2 = start(block, block, ZM)
            self.z2 = f1, f2
            self.swap(mh, zm)
            self.swap(ph, zp)
            arrived(lm, self.at(mh, zp))
            arrived(rp, self.at(ph, zm))
            self.swap(mh, zp)
            self.swap(ph, zm)

        def last_z(self):
            arrived(self.z2[0], self.at(mh, z2))
            self.swap(mh, z2)
            arrived(self.z2[1], self.at(ph, z2))
            self.swap(ph, z2)

        def whole(self):
            for handle, hv, zv in self.swaps:
                arrived(handle, self.other(hv, zv))

    pick_row = lax.broadcasted_iota(jnp.int32, (192, B), 0)
    pick_col = lax.broadcasted_iota(jnp.int32, (192, B), 1)
    ours = (pick_col == pick_row + 192 * c).astype(BF16)
    theirs = (pick_col == pick_row + 192 * oc).astype(BF16)

    class Gather:
        def __init__(self, shard, ref, k):
            self.ref, self.shard, self.k = ref, shard, k
            src = shard.at[pl.ds(mult(oc * HALF, HALF), HALF)]
            self.swapped = start(src, swap_in.at[k], OC)

        def a(self, hv, yv, lv, lo=0, n=RA):
            return self.ref.at[rows_a(hv, lo, n), cols(yv, lv)]

        def b(self, hv, yv, lv, lo=0, n=RB):
            return self.ref.at[rows_b(hv, lo, n), cols(yv, lv)]

        def both(self, block, p, m):
            return start(block, block, p), start(block, block, m)

        def first(self):
            arrived(self.swapped, swap_in.at[self.k])
            mine = self.shard[pl.ds(mult(c * HALF, HALF), HALF), :]
            block = (dot(mine, ours) + dot(swap_in[self.k], theirs)).astype(BF16)
            self.ref[rows_a(xh), cols(y, xl)] = block[:RA]
            self.ref[rows_b(xh), cols(y, xl)] = block[RA:]
            self.ax1 = self.both(self.a(xh, y, xl), XP, XM)
            self.by1 = self.both(self.b(xh, y, xl), YP, YM)

        def second(self):
            n0, n1 = SPLIT_A
            arrived(self.ax1[0], self.a(mh, y, ml))
            block = self.a(mh, y, ml, 0, n0)
            f1 = start(block, block, XP)
            arrived(self.ax1[1], self.a(ph, y, pll))
            block = self.a(ph, y, pll, n0, n1)
            f2 = start(block, block, XM)
            self.ax2 = f1, f2
            n0, n1 = SPLIT_B
            arrived(self.by1[0], self.b(xh, ym, xl))
            block = self.b(xh, ym, xl, 0, n0)
            f1 = start(block, block, YP)
            arrived(self.by1[1], self.b(xh, yp, xl))
            block = self.b(xh, yp, xl, n0, n1)
            f2 = start(block, block, YM)
            self.by2 = f1, f2

        def third(self):
            n0, n1 = SPLIT_A
            arrived(self.ax2[0], self.a(1 - xh, y, xl, 0, n0))
            arrived(self.ax2[1], self.a(1 - xh, y, xl, n0, n1))
            block = self.ref.at[pl.ds(0, 2 * RA), line(y)]
            self.ay1 = self.both(block, YP, YM)
            n0, n1 = SPLIT_B
            arrived(self.by2[0], self.b(xh, y2, xl, 0, n0))
            arrived(self.by2[1], self.b(xh, y2, xl, n0, n1))
            self.bx1 = [self.both(self.b(xh, yv, xl), XP, XM) for yv in range(4)]

        def fourth(self):
            arrived(self.ay1[0], self.ref.at[pl.ds(0, 2 * RA), line(ym)])
            block = self.ref.at[pl.ds(0, RA), line(ym)]
            f1 = start(block, block, YP)
            arrived(self.ay1[1], self.ref.at[pl.ds(0, 2 * RA), line(yp)])
            block = self.ref.at[pl.ds(RA, RA), line(yp)]
            f2 = start(block, block, YM)
            self.ay2 = f1, f2
            self.bx2 = []
            for yv in range(4):
                from_m, from_p = self.b(mh, yv, ml), self.b(ph, yv, pll)
                arrived(self.bx1[yv][0], from_m)
                arrived(self.bx1[yv][1], from_p)
                if yv < 2:
                    self.bx2.append(start(from_m, from_m, XP))
                else:
                    self.bx2.append(start(from_p, from_p, XM))

        def whole(self):
            arrived(self.ay2[0], self.ref.at[pl.ds(0, RA), line(y2)])
            arrived(self.ay2[1], self.ref.at[pl.ds(RA, RA), line(y2)])
            for yv in range(4):
                arrived(self.bx2[yv], self.b(1 - xh, yv, xl))

    class Plane:
        def __init__(self, ref, k, result):
            self.ref, self.k, self.result = ref, k, result

        def add(self, rows, columns, *parts):
            total = self.ref[rows, columns].astype(F32)
            for part in parts:
                total = total + part.astype(F32)
            self.ref[rows, columns] = total.astype(BF16)

        def a1(self):
            k = self.k
            self.sa1 = (
                start(self.ref.at[pl.ds(0, RA), line(y2)], ra1.at[k, 0], YP),
                start(self.ref.at[pl.ds(RA, RA), line(y2)], ra1.at[k, 1], YM),
            )

        def a2(self):
            k = self.k
            arrived(self.sa1[0], ra1.at[k, 0])
            self.add(pl.ds(0, RA), line(yp), ra1[k, 0])
            s1 = start(self.ref.at[pl.ds(0, 2 * RA), line(yp)], ra2.at[k, 0], YP)
            arrived(self.sa1[1], ra1.at[k, 1])
            self.add(pl.ds(RA, RA), line(ym), ra1[k, 1])
            s2 = start(self.ref.at[pl.ds(0, 2 * RA), line(ym)], ra2.at[k, 1], YM)
            self.sa2 = s1, s2

        def a3(self):
            k = self.k
            arrived(self.sa2[0], ra2.at[k, 0])
            arrived(self.sa2[1], ra2.at[k, 1])
            self.add(pl.ds(0, 2 * RA), line(y), ra2[k, 0], ra2[k, 1])
            n0, n1 = SPLIT_A
            self.sa3 = (
                start(self.ref.at[rows_a(1 - xh, 0, n0), cols(y, xl)], ra3.at[k, 0, pl.ds(0, n0)], XP),
                start(self.ref.at[rows_a(1 - xh, n0, n1), cols(y, xl)], ra3.at[k, 1, pl.ds(0, n1)], XM),
            )

        def a4(self):
            k = self.k
            n0, n1 = SPLIT_A
            arrived(self.sa3[0], ra3.at[k, 0, pl.ds(0, n0)])
            self.add(rows_a(ph, 0, n0), cols(y, pll), ra3[k, 0, :n0])
            s1 = start(self.ref.at[rows_a(ph), cols(y, pll)], ra4.at[k, 0], XP)
            arrived(self.sa3[1], ra3.at[k, 1, pl.ds(0, n1)])
            self.add(rows_a(mh, n0, n1), cols(y, ml), ra3[k, 1, :n1])
            s2 = start(self.ref.at[rows_a(mh), cols(y, ml)], ra4.at[k, 1], XM)
            self.sa4 = s1, s2

        def b1(self):
            k = self.k
            self.sb1 = [
                start(self.ref.at[rows_b(1 - xh), cols(yv, xl)], rb1.at[k, yv], XP if yv < 2 else XM)
                for yv in range(4)
            ]

        def b2(self):
            k = self.k
            for yv in range(4):
                arrived(self.sb1[yv], rb1.at[k, yv])
                hv, lv = (ph, pll) if yv < 2 else (mh, ml)
                self.add(rows_b(hv), cols(yv, lv), rb1[k, yv])
            self.sb2 = [
                (
                    start(self.ref.at[rows_b(ph), cols(yv, pll)], rb2.at[k, 0, yv], XP),
                    start(self.ref.at[rows_b(mh), cols(yv, ml)], rb2.at[k, 1, yv], XM),
                )
                for yv in range(4)
            ]

        def b3(self):
            k = self.k
            for yv in range(4):
                arrived(self.sb2[yv][0], rb2.at[k, 0, yv])
                arrived(self.sb2[yv][1], rb2.at[k, 1, yv])
                self.add(rows_b(xh), cols(yv, xl), rb2[k, 0, yv], rb2[k, 1, yv])
            n0, n1 = SPLIT_B
            self.sb3 = (
                start(self.ref.at[rows_b(xh, 0, n0), cols(y2, xl)], rb3.at[k, 0, pl.ds(0, n0)], YP),
                start(self.ref.at[rows_b(xh, n0, n1), cols(y2, xl)], rb3.at[k, 1, pl.ds(0, n1)], YM),
            )

        def b4(self):
            k = self.k
            n0, n1 = SPLIT_B
            arrived(self.sb3[0], rb3.at[k, 0, pl.ds(0, n0)])
            self.add(rows_b(xh, 0, n0), cols(yp, xl), rb3[k, 0, :n0])
            s1 = start(self.ref.at[rows_b(xh), cols(yp, xl)], rb4.at[k, 0], YP)
            arrived(self.sb3[1], rb3.at[k, 1, pl.ds(0, n1)])
            self.add(rows_b(xh, n0, n1), cols(ym, xl), rb3[k, 1, :n1])
            s2 = start(self.ref.at[rows_b(xh), cols(ym, xl)], rb4.at[k, 1], YM)
            self.sb4 = s1, s2

        def done(self):
            k = self.k
            arrived(self.sa4[0], ra4.at[k, 0])
            arrived(self.sa4[1], ra4.at[k, 1])
            arrived(self.sb4[0], rb4.at[k, 0])
            arrived(self.sb4[1], rb4.at[k, 1])
            own = self.ref[rows_a(xh), cols(y, xl)].astype(F32)
            total_a = (own + ra4[k, 0].astype(F32) + ra4[k, 1].astype(F32)).astype(BF16)
            own = self.ref[rows_b(xh), cols(y, xl)].astype(F32)
            total_b = (own + rb4[k, 0].astype(F32) + rb4[k, 1].astype(F32)).astype(BF16)
            mine = pl.ds(mult(c * HALF, HALF), HALF)
            swap_out[k, 0:RA, :] = dot_nt(total_a, theirs).astype(BF16)
            swap_out[k, RA:HALF, :] = dot_nt(total_b, theirs).astype(BF16)
            self.last = start(swap_out.at[k], self.result.at[mine], OC)
            self.result[pl.ds(mult(c * HALF, 16), RA), :] = dot_nt(total_a, ours).astype(BF16)
            self.result[pl.ds(mult(c * HALF + RA, 16), RB), :] = dot_nt(total_b, ours).astype(BF16)

        def whole(self):
            arrived(self.last, self.result.at[pl.ds(mult(oc * HALF, HALF), HALF)])

    class Grad:
        def __init__(self, ref, loc, rsw, rza, rzb, result, half):
            self.ref, self.loc, self.rsw, self.rza, self.rzb = ref, loc, rsw, rza, rzb
            self.result, self.half = result, half
            self.swaps = {}

        def at(self, hv, zv):
            return self.loc(self.ref, hv, zv, c)

        def add(self, hv, zv, *parts):
            where = self.at(hv, zv)
            total = where[...].astype(F32)
            for part in parts:
                total = total + part.astype(F32)
            where[...] = total.astype(BF16)

        def swap(self, j, zv):
            for hv in range(2):
                src = self.loc(self.ref, hv, zv, oc)
                self.swaps[j, hv] = start(src, self.rsw.at[j, hv], OC)

        def swapped(self, j, zv):
            for hv in range(2):
                arrived(self.swaps[j, hv], self.rsw.at[j, hv])
                self.add(hv, zv, self.rsw[j, hv])

        def z1(self):
            self.s1 = (
                start(self.at(0, z2), self.rza.at[0], ZP),
                start(self.at(1, z2), self.rza.at[1], ZM),
            )

        def z2(self):
            arrived(self.s1[0], self.rza.at[0])
            self.add(0, zp, self.rza[0])
            arrived(self.s1[1], self.rza.at[1])
            self.add(1, zm, self.rza[1])
            self.s2 = [
                (
                    start(self.at(hv, zp), self.rzb.at[0, hv], ZP),
                    start(self.at(hv, zm), self.rzb.at[1, hv], ZM),
                )
                for hv in range(2)
            ]

        def x(self):
            for hv in range(2):
                arrived(self.s2[hv][0], self.rzb.at[0, hv])
                arrived(self.s2[hv][1], self.rzb.at[1, hv])
                self.add(hv, z, self.rzb[0, hv], self.rzb[1, hv])
            self.s3 = (
                start(self.at(ph, z), self.half(self.result, xh), XP),
                start(self.at(mh, z), self.half(self.result, xh), XM),
            )

        def whole(self):
            arrived(self.s3[0], self.half(self.result, mh))
            arrived(self.s3[1], self.half(self.result, ph))

    def half1(ref, hv):
        return ref.at[:, pl.ds(mult(hv * B, 128), B)]

    def half2(ref, hv):
        return ref.at[pl.ds(mult(hv * B, 128), B), :]

    def transpose_tokens():
        @pl.loop(0, D // 256)
        def _(j):
            at = pl.ds(mult(j * 256, 256), 256)
            tok_t[at, :] = tok[:, at].T

    def hidden():
        @pl.loop(0, HID // 256)
        def _(j):
            at = pl.ds(mult(j * 256, 256), 256)
            for lo in range(0, TOK, 256):
                rows = pl.ds(lo, 256)
                pre = dot(tok[rows, :], w1[:, at])
                cdf = 0.5 * (1.0 + lax.erf(pre * inv_root_two))
                value = (pre * cdf).astype(BF16)
                act[rows, at] = value
                act_t[at, rows] = value.T
                slope[rows, at] = cdf + pre * jnp.exp(-0.5 * pre * pre) * inv_root_tau

    def output_terms(yv):
        oterm[:, line(yv)] = dot(act[...], w2[:, line(yv)]).astype(BF16)

    def second_terms(zv):
        for hv in range(2):
            at = pl.ds(mult((hv * 4 + zv) * B, 128), B)
            p2[:, at] = dot(act_t[...], cot[:, at]).astype(BF16)

    def hidden_grad():
        @pl.loop(0, HID // 256)
        def _(j):
            at = pl.ds(mult(j * 256, 256), 256)
            for lo in range(0, TOK, 256):
                rows = pl.ds(lo, 256)
                back = dot_nt(cot[rows, :], w2[at, :])
                hg[rows, at] = (back * slope[rows, at]).astype(BF16)

    def first_terms(zv):
        for hv in range(2):
            at = pl.ds(mult((hv * 4 + zv) * B, 128), B)
            p1[at, :] = dot(tok_t[at, :], hg[...]).astype(BF16)

    def input_terms(yv):
        tok[:, line(yv)] = dot_nt(hg[...], w1[line(yv), :]).astype(BF16)

    first = Weights(w1_in, w1, loc1, half1)
    gt = Gather(tok_in, tok, 0)
    gc = Gather(cot_in, cot, 1)
    gt.first()
    first.along_z()
    second = Weights(w2_in, w2, loc2, half2)
    gt.second()
    gt.third()
    gc.first()
    first.forward_z()
    gt.fourth()
    gc.second()
    gc.third()
    gt.whole()
    first.last_z()
    second.along_z()
    transpose_tokens()
    first.whole()
    hidden()
    second.forward_z()
    gc.fourth()
    second.last_z()
    gc.whole()
    second.whole()
    links.flush()

    po = Plane(oterm, 0, out_ref)
    pi = Plane(tok, 1, ing_ref)
    gs = Grad(p2, loc2, rsw2, rza2, rzb2, g2_ref, half2)
    gf = Grad(p1, loc1, rsw1, rza1, rzb1, g1_ref, half1)

    output_terms(y2)
    po.a1()
    second_terms(z2)
    gs.swap(0, z2)
    for yv in (yp, ym, y):
        output_terms(yv)
    po.b1()
    second_terms(zp)
    gs.swap(1, zp)
    gs.swapped(0, z2)
    gs.z1()
    second_terms(zm)
    gs.swap(2, zm)
    second_terms(z)
    gs.swap(3, z)
    gs.swapped(1, zp)
    gs.swapped(2, zm)
    po.a2()
    po.b2()
    gs.z2()
    hidden_grad()
    first_terms(z2)
    gf.swap(0, z2)
    gs.swapped(3, z)
    input_terms(y2)
    pi.a1()
    first_terms(zp)
    gf.swap(1, zp)
    first_terms(zm)
    gf.swap(2, zm)
    gf.swapped(0, z2)
    gf.z1()
    for yv in (yp, ym, y):
        input_terms(yv)
    pi.b1()
    first_terms(z)
    gf.swap(3, z)
    po.a3()
    po.b3()
    gf.swapped(1, zp)
    gf.swapped(2, zm)
    gf.swapped(3, z)
    pi.a2()
    pi.b2()
    gs.x()
    gf.z2()
    po.a4()
    po.b4()
    po.done()
    pi.a3()
    pi.b3()
    pi.a4()
    pi.b4()
    gf.x()
    pi.done()
    for part in (po, gs, gf, pi):
        part.whole()
    links.flush()


def shards(tokens, w_first, w_second, cotangent):
    vmem = pl.BlockSpec(memory_space=pltpu.VMEM)
    hbm = pl.BlockSpec(memory_space=pl.ANY)
    outputs, input_grad, first_grad, second_grad = pl.pallas_call(
        kernel,
        name="mlp",
        out_shape=(
            jax.ShapeDtypeStruct((TOK, 192), BF16),
            jax.ShapeDtypeStruct((TOK, 192), BF16),
            jax.ShapeDtypeStruct((B, 2 * B), BF16),
            jax.ShapeDtypeStruct((2 * B, B), BF16),
        ),
        in_specs=[vmem, vmem, hbm, hbm],
        out_specs=(vmem, vmem, hbm, hbm),
        scratch_shapes=[
            pltpu.VMEM((D, HID), BF16),
            pltpu.VMEM((HID, D), BF16),
            pltpu.VMEM((TOK, D), BF16),
            pltpu.VMEM((TOK, D), BF16),
            pltpu.VMEM((D, TOK), BF16),
            pltpu.VMEM((TOK, HID), BF16),
            pltpu.VMEM((HID, TOK), BF16),
            pltpu.VMEM((TOK, HID), F32),
            pltpu.VMEM((TOK, HID), BF16),
            pltpu.VMEM((TOK, D), BF16),
            pltpu.VMEM((D, HID), BF16),
            pltpu.VMEM((HID, D), BF16),
            pltpu.VMEM((4, 2, B, B), BF16),
            pltpu.VMEM((4, 2, B, B), BF16),
            pltpu.VMEM((2, B, B), BF16),
            pltpu.VMEM((2, B, B), BF16),
            pltpu.VMEM((2, 2, B, B), BF16),
            pltpu.VMEM((2, 2, B, B), BF16),
            pltpu.VMEM((2, 2, RA, 2 * B), BF16),
            pltpu.VMEM((2, 2, 2 * RA, 2 * B), BF16),
            pltpu.VMEM((2, 2, SPLIT_A[0], B), BF16),
            pltpu.VMEM((2, 2, RA, B), BF16),
            pltpu.VMEM((2, 4, RB, B), BF16),
            pltpu.VMEM((2, 2, 4, RB, B), BF16),
            pltpu.VMEM((2, 2, SPLIT_B[0], B), BF16),
            pltpu.VMEM((2, 2, RB, B), BF16),
            pltpu.VMEM((2, HALF, 192), BF16),
            pltpu.VMEM((2, HALF, 192), BF16),
            pltpu.SemaphoreType.DMA((NSEM,)),
            pltpu.SemaphoreType.DMA((NSEM,)),
        ],
        compiler_params=pltpu.CompilerParams(
            collective_id=0, has_side_effects=True, vmem_limit_bytes=60 * 1024 * 1024
        ),
        cost_estimate=pl.CostEstimate(flops=14_500_000_000, bytes_accessed=40_000_000, transcendentals=800_000),
    )(tokens, cotangent, w_first, w_second)
    return outputs, input_grad, first_grad.astype(F32), second_grad.astype(F32)


def solution(mesh):
    finer = Mesh(mesh.devices.reshape(2, 4, 4, 2, 2), AXES)
    in_specs = (P(DP, MP), P(DP, MP), P(MP, DP), P(DP, MP))
    out_specs = (P(DP, MP), P(DP, MP), P(DP, MP), P(MP, DP))
    return jax.shard_map(
        shards, mesh=finer, in_specs=in_specs, out_specs=out_specs, check_vma=False
    )
```

```python
import jax
import jax.numpy as jnp
from jax import lax
from jax.experimental import pallas as pl
from jax.experimental.pallas import tpu as pltpu
from jax.sharding import Mesh
from jax.sharding import PartitionSpec as P

AXES = ("xh", "z", "y", "xl", "c")
DP = ("xh", "z")
MP = ("y", "xl", "c")
MESH = pl.DeviceIdType.MESH
F32 = jnp.float32
BF16 = jnp.bfloat16

D = 3072
B = 384
HID = 768
TOK = 512
HALF = 256
RA = 176
RB = HALF - RA
SPLIT_A = (96, 80)
SPLIT_B = (48, 32)
NSEM = 240

inv_root_two = 0.7071067811865476
inv_root_tau = 0.3989422804014327


def dot(a, b):
    return jnp.dot(a, b, preferred_element_type=F32)


def dot_nt(a, b):
    return lax.dot_general(a, b, (((1,), (1,)), ((), ())), preferred_element_type=F32)


def dot_tn(a, b):
    return lax.dot_general(a, b, (((0,), (0,)), ((), ())), preferred_element_type=F32)


def mult(value, of):
    return pl.multiple_of(value, of)


class Links:
    def __init__(self, send, recv):
        self.send, self.recv, self.count, self.open = send, recv, 0, []

    def start(self, src, dst, peer):
        i = self.count
        self.count += 1
        copy = pltpu.make_async_remote_copy(
            src_ref=src,
            dst_ref=dst,
            send_sem=self.send.at[i],
            recv_sem=self.recv.at[i],
            device_id=peer,
            device_id_type=MESH,
        )
        copy.start()
        self.open.append((src, copy))
        return (i, peer)

    def arrived(self, handle, where):
        i, peer = handle
        pltpu.make_async_remote_copy(
            src_ref=where,
            dst_ref=where,
            send_sem=self.send.at[i],
            recv_sem=self.recv.at[i],
            device_id=peer,
            device_id_type=MESH,
        ).wait_recv()

    def flush(self, ref=None):
        kept = []
        for src, copy in self.open:
            if ref is None or getattr(src, "ref", src) is ref:
                copy.wait_send()
            else:
                kept.append((src, copy))
        self.open = kept


def kernel(
    tok_in, cot_in, w1_in, w2_in,
    out_ref, ing_ref, g1_ref, g2_ref,
    w1, w2, tok, cot, tok_t, act, act_t, slope, hg, oterm, p1, p2,
    rsw1, rsw2, rza1, rza2, rzb1, rzb2,
    ra1, ra2, ra3, ra4, rb1, rb2, rb3, rb4,
    swap_in, swap_out, stage, send, recv, local,
):
    xh, z, y, xl, c = (lax.axis_index(a) for a in AXES)
    x = xh * 2 + xl
    xp, xm = lax.rem(x + 1, 4), lax.rem(x + 3, 4)
    ph, pll = xp // 2, lax.rem(xp, 2)
    mh, ml = xm // 2, lax.rem(xm, 2)
    yp, ym, y2 = lax.rem(y + 1, 4), lax.rem(y + 3, 4), lax.rem(y + 2, 4)
    zp, zm, z2 = lax.rem(z + 1, 4), lax.rem(z + 3, 4), lax.rem(z + 2, 4)
    oc = 1 - c
    XP, XM = {"xh": ph, "xl": pll}, {"xh": mh, "xl": ml}
    YP, YM, ZP, ZM, OC = {"y": yp}, {"y": ym}, {"z": zp}, {"z": zm}, {"c": oc}
    H = B // 2
    OWN, OTHER = 0, 1
    own_h, other_h = xh, 1 - xh
    links = Links(send, recv)
    start, arrived = links.start, links.arrived

    bar = pltpu.get_barrier_semaphore()
    for peer in (XP, XM, YP, YM, ZP, ZM, OC):
        pl.semaphore_signal(bar, inc=1, device_id=peer, device_id_type=MESH)
    pl.semaphore_wait(bar, 7)

    def rows_a(hv, lo=0, n=RA):
        return pl.ds(mult(hv * RA + lo, 16), n)

    def rows_b(hv, lo=0, n=RB):
        return pl.ds(mult(2 * RA + hv * RB + lo, 16), n)

    def cols(yv, lv):
        return pl.ds(mult((yv * 2 + lv) * B, 128), B)

    def line(yv):
        return pl.ds(mult(yv * 2 * B, 128), 2 * B)

    def loc1(ref, hv, zv, cv, lo=0, n=B):
        return ref.at[pl.ds(mult((hv * 4 + zv) * B + lo, 64), n), pl.ds(mult(cv * B, 128), B)]

    def loc2(ref, hv, zv, cv, lo=0, n=B):
        return ref.at[pl.ds(mult(cv * B + lo, 64), n), pl.ds(mult((hv * 4 + zv) * B, 128), B)]

    def half1(ref, hv, lo=0, n=B):
        return ref.at[pl.ds(lo, n), pl.ds(mult(hv * B, 128), B)]

    def half2(ref, hv, lo=0, n=B):
        return ref.at[pl.ds(mult(hv * B + lo, 64), n), :]

    class Weights:
        def __init__(self, k, shard, ref, loc, half):
            self.at = lambda b, zv, *part: loc(ref, (own_h, other_h)[b], zv, c, *part)
            self.other = lambda b, zv: loc(ref, (own_h, other_h)[b], zv, oc)
            self.relayed = lambda hv, *part: loc(ref, hv, z, c, *part)
            self.swaps, self.z1, self.z2 = [], {}, {}
            self.k, self.shard, self.half = k, shard, half

        def swap(self, b, zv, src=None):
            block = self.at(b, zv)
            self.swaps.append((start(block if src is None else src, block, OC), b, zv))

        def exchange(self):
            self.x1 = tuple(
                start(self.half(self.shard, other_h, lo, H), stage.at[self.k, i], peer)
                for i, (lo, peer) in enumerate(((0, XP), (H, XM)))
            )

        def relay(self):
            arrived(self.x1[0], stage.at[self.k, 0])
            s0 = start(stage.at[self.k, 0], self.relayed(mh, 0, H), XP)
            arrived(self.x1[1], stage.at[self.k, 1])
            s1 = start(stage.at[self.k, 1], self.relayed(ph, H, H), XM)
            self.x2 = s0, s1

        def own(self):
            src, dst = self.half(self.shard, own_h), self.at(OWN, z)
            self.z1[OWN] = start(src, dst, ZP), start(src, dst, ZM)
            self.swap(OWN, z, src)
            self.copy = pltpu.make_async_copy(src, dst, local.at[self.k])
            self.copy.start()

        def partner(self):
            block = self.at(OTHER, z)
            arrived(self.x2[0], self.at(OTHER, z, 0, H))
            arrived(self.x2[1], self.at(OTHER, z, H, H))
            self.z1[OTHER] = start(block, block, ZP), start(block, block, ZM)
            self.swap(OTHER, z)

        def forward(self, b):
            p, m = self.z1[b]
            from_m, from_p = self.at(b, zm), self.at(b, zp)
            if b == OWN:
                arrived(p, from_m)
                self.z2[b] = start(from_m, from_m, ZP)
                arrived(m, from_p)
            else:
                arrived(m, from_p)
                self.z2[b] = start(from_p, from_p, ZM)
                arrived(p, from_m)
            self.swap(b, zm)
            self.swap(b, zp)

        def last(self, b):
            arrived(self.z2[b], self.at(b, z2))
            self.swap(b, z2)

        def whole(self):
            self.copy.wait()
            for handle, b, zv in self.swaps:
                arrived(handle, self.other(b, zv))

    xs = {"o": (xh, xl), "m": (mh, ml), "p": (ph, pll), "t": (1 - xh, xl)}
    ys = {"o": y, "m": ym, "p": yp, "t": y2}
    PLUS = "om"

    def place_a(ref, i, j, lo=0, n=RA):
        (hv, lv), yv = xs[i], ys[j]
        return ref.at[rows_a(hv, lo, n), cols(yv, lv)]

    def place_b(ref, i, j, lo=0, n=RB):
        (hv, lv), yv = xs[j], ys[i]
        return ref.at[rows_b(hv, lo, n), cols(yv, lv)]

    ROUTES = {"a": (place_a, SPLIT_A, (XP, XM), (YP, YM)), "b": (place_b, SPLIT_B, (YP, YM), (XP, XM))}

    pick_row = lax.broadcasted_iota(jnp.int32, (192, B), 0)
    pick_col = lax.broadcasted_iota(jnp.int32, (192, B), 1)
    ours = (pick_col == pick_row + 192 * c).astype(BF16)
    theirs = (pick_col == pick_row + 192 * oc).astype(BF16)

    class GatherPart:
        def __init__(self, ref, route):
            place, self.split, self.first, self.second = ROUTES[route]
            self.at = lambda *where: place(ref, *where)
            self.f2, self.s1, self.s2 = {}, {}, {}

        def both(self, i):
            block = self.at(i, "o")
            self.s1[i] = tuple(start(block, block, peer) for peer in self.second)

        def own_first(self):
            block = self.at("o", "o")
            self.f1 = tuple(start(block, block, peer) for peer in self.first)

        def near(self, i):
            n0, n1 = self.split
            p, m = self.first
            if i == "m":
                arrived(self.f1[0], self.at("m", "o"))
                block = self.at("m", "o", 0, n0)
                self.f2[0] = start(block, block, p)
            else:
                arrived(self.f1[1], self.at("p", "o"))
                block = self.at("p", "o", n0, n1)
                self.f2[1] = start(block, block, m)
            self.both(i)

        def far(self):
            n0, n1 = self.split
            arrived(self.f2[0], self.at("t", "o", 0, n0))
            arrived(self.f2[1], self.at("t", "o", n0, n1))
            self.both("t")

        def forward(self, i):
            from_m, from_p = self.at(i, "m"), self.at(i, "p")
            if i in PLUS:
                arrived(self.s1[i][0], from_m)
                self.s2[i] = start(from_m, from_m, self.second[0])
                arrived(self.s1[i][1], from_p)
            else:
                arrived(self.s1[i][1], from_p)
                self.s2[i] = start(from_p, from_p, self.second[1])
                arrived(self.s1[i][0], from_m)

        def whole(self):
            for i in "ompt":
                arrived(self.s2[i], self.at(i, "t"))

    class Gather:
        def __init__(self, shard, ref, k):
            self.ref, self.shard, self.k = ref, shard, k
            self.a, self.b = GatherPart(ref, "a"), GatherPart(ref, "b")

        def swap(self):
            src = self.shard.at[:, pl.ds(mult(oc * HALF, HALF), HALF)]
            self.swapped = start(src, swap_in.at[self.k], OC)

        def assemble(self):
            arrived(self.swapped, swap_in.at[self.k])
            mine = self.shard[:, pl.ds(mult(c * HALF, HALF), HALF)]
            block = (dot_tn(mine, ours) + dot_tn(swap_in[self.k], theirs)).astype(BF16)
            self.ref[rows_a(xh), cols(y, xl)] = block[:RA]
            self.ref[rows_b(xh), cols(y, xl)] = block[RA:]

        def whole(self):
            self.a.whole()
            self.b.whole()

        def flush(self):
            links.flush(self.ref)

    def add_into(where, *parts):
        total = where[...].astype(F32)
        for part in parts:
            total = total + part.astype(F32)
        where[...] = total.astype(BF16)

    class SumPart:
        def __init__(self, ref, route, k, r1, r2, r3, r4):
            place, self.split, self.first, self.second = ROUTES[route]
            self.at = lambda *where: place(ref, *where)
            self.r1, self.r2, self.r3, self.r4 = r1.at[k], r2.at[k], r3.at[k], r4.at[k]
            self.s0, self.s1, self.s2, self.s4 = {}, {}, {}, {}

        def far(self, i):
            n = "ompt".index(i)
            peer = self.second[0] if i in PLUS else self.second[1]
            self.s1[i] = start(self.at(i, "t"), self.r1.at[n], peer)

        def early(self, i):
            n = "ompt".index(i)
            if i in PLUS:
                self.s0[i] = start(self.at(i, "m"), self.r2.at[1, n], self.second[1])
            else:
                self.s0[i] = start(self.at(i, "p"), self.r2.at[0, n], self.second[0])

        def near(self, i):
            n = "ompt".index(i)
            arrived(self.s1[i], self.r1.at[n])
            if i in PLUS:
                add_into(self.at(i, "p"), self.r1[n])
                p = start(self.at(i, "p"), self.r2.at[0, n], self.second[0])
                self.s2[i] = p, self.s0[i]
            else:
                add_into(self.at(i, "m"), self.r1[n])
                m = start(self.at(i, "m"), self.r2.at[1, n], self.second[1])
                self.s2[i] = self.s0[i], m

        def summed(self, i, wait=True):
            n = "ompt".index(i)
            if wait:
                arrived(self.s2[i][0], self.r2.at[0, n])
                arrived(self.s2[i][1], self.r2.at[1, n])
            return self.r2[0, n], self.r2[1, n]

        def first_far(self):
            add_into(self.at("t", "o"), *self.summed("t"))
            n0, n1 = self.split
            self.s3 = (
                start(self.at("t", "o", 0, n0), self.r3.at[0, pl.ds(0, n0)], self.first[0]),
                start(self.at("t", "o", n0, n1), self.r3.at[1, pl.ds(0, n1)], self.first[1]),
            )

        def first_near(self, i):
            n0, n1 = self.split
            if i == "p":
                arrived(self.s3[0], self.r3.at[0, pl.ds(0, n0)])
                add_into(self.at("p", "o", n0, n1), *(r[n0:] for r in self.summed("p")))
                add_into(self.at("p", "o", 0, n0), self.r3[0, :n0], *(r[:n0] for r in self.summed("p", False)))
                self.s4[0] = start(self.at("p", "o"), self.r4.at[0], self.first[0])
            else:
                arrived(self.s3[1], self.r3.at[1, pl.ds(0, n1)])
                add_into(self.at("m", "o", 0, n0), *(r[:n0] for r in self.summed("m")))
                add_into(self.at("m", "o", n0, n1), self.r3[1, :n1], *(r[n0:] for r in self.summed("m", False)))
                self.s4[1] = start(self.at("m", "o"), self.r4.at[1], self.first[1])

        def total(self):
            parts = self.summed("o")
            arrived(self.s4[0], self.r4.at[0])
            arrived(self.s4[1], self.r4.at[1])
            value = self.at("o", "o")[...].astype(F32)
            for part in (*parts, self.r4[0], self.r4[1]):
                value = value + part.astype(F32)
            return value.astype(BF16)

    class Plane:
        def __init__(self, ref, k, result):
            self.k, self.result = k, result
            self.a = SumPart(ref, "a", k, ra1, ra2, ra3, ra4)
            self.b = SumPart(ref, "b", k, rb1, rb2, rb3, rb4)

        def done(self):
            k = self.k
            total = jnp.concatenate([self.a.total(), self.b.total()], axis=0)
            mine = pl.ds(mult(c * HALF, HALF), HALF)
            swap_out[k] = dot_nt(theirs, total).astype(BF16)
            self.last = start(swap_out.at[k], self.result.at[:, mine], OC)
            self.result[:, mine] = dot_nt(ours, total).astype(BF16)

        def whole(self):
            arrived(self.last, self.result.at[:, pl.ds(mult(oc * HALF, HALF), HALF)])

    class Grad:
        def __init__(self, k, ref, loc, rsw, rz1, rz2, result, half):
            self.at = lambda b, zv, *part: loc(ref, (own_h, other_h)[b], zv, c, *part)
            self.theirs = lambda b, zv: loc(ref, (own_h, other_h)[b], zv, oc)
            self.k, self.rsw, self.rz1, self.rz2, self.result, self.half = k, rsw, rz1, rz2, result, half
            self.swaps, self.s0, self.s1, self.s2 = {}, {}, {}, {}

        def swap(self, j, zv):
            for b in (OTHER, OWN):
                self.swaps[j, b] = start(self.theirs(b, zv), self.rsw.at[j, b], OC)

        def swapped(self, j, zv, b):
            arrived(self.swaps[j, b], self.rsw.at[j, b])
            add_into(self.at(b, zv), self.rsw[j, b])

        def far(self, b):
            self.s1[b] = start(self.at(b, z2), self.rz1.at[b], ZP if b == OWN else ZM)

        def early(self, b):
            if b == OWN:
                self.swapped(2, zm, b)
                self.s0[b] = start(self.at(b, zm), self.rz2.at[1, b], ZM)
            else:
                self.swapped(1, zp, b)
                self.s0[b] = start(self.at(b, zp), self.rz2.at[0, b], ZP)

        def near(self, b):
            arrived(self.s1[b], self.rz1.at[b])
            j, zv = (1, zp) if b == OWN else (2, zm)
            arrived(self.swaps[j, b], self.rsw.at[j, b])
            add_into(self.at(b, zv), self.rsw[j, b], self.rz1[b])
            if b == OWN:
                self.s2[b] = start(self.at(b, zp), self.rz2.at[0, b], ZP), self.s0[b]
            else:
                self.s2[b] = self.s0[b], start(self.at(b, zm), self.rz2.at[1, b], ZM)

        def total(self, b):
            arrived(self.s2[b][0], self.rz2.at[0, b])
            arrived(self.s2[b][1], self.rz2.at[1, b])
            arrived(self.swaps[3, b], self.rsw.at[3, b])
            add_into(self.at(b, z), self.rsw[3, b], self.rz2[0, b], self.rz2[1, b])
            if b == OWN:
                self.copy = pltpu.make_async_copy(
                    self.at(b, z), self.half(self.result, own_h), local.at[self.k]
                )
                self.copy.start()
            else:
                self.s3 = tuple(
                    start(self.at(b, z, lo, H), stage.at[self.k, i], peer)
                    for i, (lo, peer) in enumerate(((0, XP), (H, XM)))
                )

        def relay(self):
            arrived(self.s3[0], stage.at[self.k, 0])
            s0 = start(stage.at[self.k, 0], self.half(self.result, mh, 0, H), XP)
            arrived(self.s3[1], stage.at[self.k, 1])
            s1 = start(stage.at[self.k, 1], self.half(self.result, ph, H, H), XM)
            self.s4 = s0, s1

        def whole(self):
            self.copy.wait()
            arrived(self.s4[0], self.half(self.result, other_h, 0, H))
            arrived(self.s4[1], self.half(self.result, other_h, H, H))

    def transpose_tokens():
        @pl.loop(0, D // 256)
        def _(j):
            at = pl.ds(mult(j * 256, 256), 256)
            tok_t[at, :] = tok[:, at].T

    def hidden(j):
        at = pl.ds(j * 256, 256)
        for lo in range(0, TOK, 256):
            rows = pl.ds(lo, 256)
            pre = dot(tok[rows, :], w1[:, at])
            cdf = 0.5 * (1.0 + lax.erf(pre * inv_root_two))
            value = (pre * cdf).astype(BF16)
            act[rows, at] = value
            act_t[at, rows] = value.T
            slope[rows, at] = cdf + pre * jnp.exp(-0.5 * pre * pre) * inv_root_tau

    def output_terms(yv):
        oterm[:, line(yv)] = dot(act[...], w2[:, line(yv)]).astype(BF16)

    def second_terms(zv):
        for hv in range(2):
            at = pl.ds(mult((hv * 4 + zv) * B, 128), B)
            p2[:, at] = dot(act_t[...], cot[:, at]).astype(BF16)

    def hidden_grad(j):
        at = pl.ds(j * 256, 256)
        for lo in range(0, TOK, 256):
            rows = pl.ds(lo, 256)
            back = dot_nt(cot[rows, :], w2[at, :])
            hg[rows, at] = (back * slope[rows, at]).astype(BF16)

    def first_terms(zv):
        for hv in range(2):
            at = pl.ds(mult((hv * 4 + zv) * B, 128), B)
            p1[at, :] = dot(tok_t[at, :], hg[...]).astype(BF16)

    def input_terms(yv):
        tok[:, line(yv)] = dot_nt(hg[...], w1[line(yv), :]).astype(BF16)

    wf = Weights(0, w1_in, w1, loc1, half1)
    ws = Weights(1, w2_in, w2, loc2, half2)
    gt = Gather(tok_in, tok, 0)
    gc = Gather(cot_in, cot, 1)
    po = Plane(oterm, 0, out_ref)
    pi = Plane(tok, 1, ing_ref)
    gs = Grad(2, p2, loc2, rsw2, rza2, rzb2, g2_ref, half2)
    gf = Grad(3, p1, loc1, rsw1, rza1, rzb1, g1_ref, half1)
    gc.swap()
    wf.own()
    wf.exchange()
    gt.swap()
    gc.assemble()
    gc.b.own_first()
    ws.own()
    gt.assemble()
    gt.b.own_first()
    gt.a.both("o")
    gc.a.both("o")
    gt.a.own_first()
    wf.relay()
    ws.exchange()
    gt.a.near("m")
    gt.a.near("p")
    wf.partner()
    wf.forward(OWN)
    ws.relay()
    gt.b.near("p")
    gc.b.near("m")
    gt.b.near("m")
    gc.a.own_first()
    gc.b.near("p")
    gt.a.far()
    gt.a.forward("m")
    ws.partner()
    gt.a.forward("p")
    ws.forward(OWN)
    gt.a.forward("o")
    wf.forward(OTHER)
    gt.b.both("o")
    gt.a.forward("t")
    gt.b.forward("m")
    gc.a.near("m")
    gc.a.near("p")
    gt.b.far()
    wf.last(OWN)
    gc.b.both("o")
    gt.b.forward("t")
    gt.b.forward("o")
    gt.b.forward("p")
    gc.a.far()
    ws.forward(OTHER)
    gc.a.forward("p")
    gc.b.far()
    gc.b.forward("p")
    gc.a.forward("o")
    wf.last(OTHER)
    gc.b.forward("o")
    gc.b.forward("m")
    gt.whole()
    transpose_tokens()
    wf.whole()
    gc.a.forward("m")
    gc.b.forward("t")
    gc.a.forward("t")
    hidden(1)
    gt.flush()
    hidden(2)
    ws.last(OWN)
    ws.last(OTHER)
    hidden(0)
    ws.whole()
    output_terms(y2)
    gc.whole()
    po.a.far("t")
    po.a.far("m")
    second_terms(z2)
    gs.swap(0, z2)
    po.b.far("t")
    po.b.early("t")
    po.a.far("p")
    output_terms(ym)
    po.b.far("m")
    output_terms(yp)
    po.b.far("p")
    po.a.early("t")
    po.b.early("m")
    gs.swapped(0, z2, OTHER)
    po.b.early("p")
    po.a.early("p")
    gs.far(OTHER)
    gs.swapped(0, z2, OWN)
    gs.far(OWN)
    hidden_grad(2)
    hidden_grad(0)
    po.a.near("t")
    po.b.near("m")
    po.b.near("t")
    hidden_grad(1)
    first_terms(z2)
    po.b.near("p")
    gf.swap(0, z2)
    input_terms(y2)
    po.b.first_far()
    po.a.early("m")
    pi.b.early("t")
    pi.b.far("t")
    output_terms(y)
    gf.swapped(0, z2, OTHER)
    gf.swapped(0, z2, OWN)
    gf.far(OWN)
    po.b.early("o")
    po.b.far("o")
    po.a.near("p")
    gf.far(OTHER)
    po.a.near("m")
    first_terms(zm)
    po.a.first_far()
    gf.swap(2, zm)
    second_terms(zp)
    gs.swap(1, zp)
    pi.b.near("t")
    po.b.first_near("p")
    input_terms(ym)
    pi.b.far("m")
    pi.a.far("m")
    second_terms(zm)
    gs.early(OTHER)
    gs.swap(2, zm)
    po.b.near("o")
    first_terms(zp)
    pi.b.early("m")
    pi.b.first_far()
    pi.a.far("o")
    pi.b.near("m")
    po.a.first_near("m")
    gs.near(OTHER)
    pi.a.far("t")
    gf.swap(1, zp)
    input_terms(yp)
    pi.b.early("p")
    input_terms(y)
    pi.b.far("o")
    first_terms(z)
    po.b.first_near("m")
    pi.b.first_near("m")
    po.a.first_near("p")
    pi.b.far("p")
    pi.a.early("t")
    gf.swap(3, z)
    gf.early(OTHER)
    pi.b.early("o")
    pi.a.near("t")
    second_terms(z)
    gs.swap(3, z)
    po.a.far("o")
    pi.a.far("p")
    pi.b.near("o")
    gf.near(OTHER)
    gf.early(OWN)
    gs.early(OWN)
    pi.b.near("p")
    gs.total(OTHER)
    pi.a.early("m")
    pi.b.first_near("p")
    pi.a.first_far()
    pi.a.near("m")
    gf.near(OWN)
    pi.a.early("p")
    gs.relay()
    pi.a.near("p")
    po.a.early("o")
    gf.total(OTHER)
    po.a.near("o")
    pi.a.first_near("m")
    pi.a.early("o")
    pi.a.near("o")
    gs.near(OWN)
    pi.a.first_near("p")
    gf.relay()
    po.done()
    pi.done()
    gf.total(OWN)
    gs.total(OWN)
    for part in (po, gs, gf, pi):
        part.whole()
    links.flush()


def shards(tokens, w_first, w_second, cotangent):
    vmem = pl.BlockSpec(memory_space=pltpu.VMEM)
    hbm = pl.BlockSpec(memory_space=pl.ANY)
    outputs, input_grad, first_grad, second_grad = pl.pallas_call(
        kernel,
        name="mlp",
        out_shape=(
            jax.ShapeDtypeStruct((192, TOK), BF16),
            jax.ShapeDtypeStruct((192, TOK), BF16),
            jax.ShapeDtypeStruct((B, 2 * B), BF16),
            jax.ShapeDtypeStruct((2 * B, B), BF16),
        ),
        in_specs=[vmem, vmem, hbm, hbm],
        out_specs=(vmem, vmem, hbm, hbm),
        scratch_shapes=[
            pltpu.VMEM((D, HID), BF16),
            pltpu.VMEM((HID, D), BF16),
            pltpu.VMEM((TOK, D), BF16),
            pltpu.VMEM((TOK, D), BF16),
            pltpu.VMEM((D, TOK), BF16),
            pltpu.VMEM((TOK, HID), BF16),
            pltpu.VMEM((HID, TOK), BF16),
            pltpu.VMEM((TOK, HID), F32),
            pltpu.VMEM((TOK, HID), BF16),
            pltpu.VMEM((TOK, D), BF16),
            pltpu.VMEM((D, HID), BF16),
            pltpu.VMEM((HID, D), BF16),
            pltpu.VMEM((4, 2, B, B), BF16),
            pltpu.VMEM((4, 2, B, B), BF16),
            pltpu.VMEM((2, B, B), BF16),
            pltpu.VMEM((2, B, B), BF16),
            pltpu.VMEM((2, 2, B, B), BF16),
            pltpu.VMEM((2, 2, B, B), BF16),
            pltpu.VMEM((2, 4, RA, B), BF16),
            pltpu.VMEM((2, 2, 4, RA, B), BF16),
            pltpu.VMEM((2, 2, SPLIT_A[0], B), BF16),
            pltpu.VMEM((2, 2, RA, B), BF16),
            pltpu.VMEM((2, 4, RB, B), BF16),
            pltpu.VMEM((2, 2, 4, RB, B), BF16),
            pltpu.VMEM((2, 2, SPLIT_B[0], B), BF16),
            pltpu.VMEM((2, 2, RB, B), BF16),
            pltpu.VMEM((2, 192, HALF), BF16),
            pltpu.VMEM((2, 192, HALF), BF16),
            pltpu.VMEM((4, 2, B // 2, B), BF16),
            pltpu.SemaphoreType.DMA((NSEM,)),
            pltpu.SemaphoreType.DMA((NSEM,)),
            pltpu.SemaphoreType.DMA((4,)),
        ],
        compiler_params=pltpu.CompilerParams(
            collective_id=0, has_side_effects=True, vmem_limit_bytes=60 * 1024 * 1024
        ),
        cost_estimate=pl.CostEstimate(flops=14_500_000_000, bytes_accessed=40_000_000, transcendentals=800_000),
    )(tokens.T, cotangent.T, w_first, w_second)
    return outputs.T, input_grad.T, first_grad.astype(F32), second_grad.astype(F32)


def solution(mesh):
    finer = Mesh(mesh.devices.reshape(2, 4, 4, 2, 2), AXES)
    in_specs = (P(DP, MP), P(DP, MP), P(MP, DP), P(DP, MP))
    out_specs = (P(DP, MP), P(DP, MP), P(DP, MP), P(MP, DP))
    return jax.shard_map(
        shards, mesh=finer, in_specs=in_specs, out_specs=out_specs, check_vma=False
    )
```

```python
import jax
import jax.numpy as jnp
from jax import lax
from jax.experimental import pallas as pl
from jax.experimental.pallas import tpu as pltpu
from jax.sharding import Mesh
from jax.sharding import PartitionSpec as P

AXES = ("xh", "z", "y", "xl", "c")
DP = ("xh", "z")
MP = ("y", "xl", "c")
MESH = pl.DeviceIdType.MESH
F32 = jnp.float32
BF16 = jnp.bfloat16

D = 3072
B = 384
HID = 768
TOK = 512
HALF = 256
RA = 176
RB = HALF - RA
SPLIT_A = (96, 80)
SPLIT_B = (48, 32)
NSEM = 204

inv_root_two = 0.7071067811865476
inv_root_tau = 0.3989422804014327


def dot(a, b):
    return jnp.dot(a, b, preferred_element_type=F32)


def dot_nt(a, b):
    return lax.dot_general(a, b, (((1,), (1,)), ((), ())), preferred_element_type=F32)


def dot_tn(a, b):
    return lax.dot_general(a, b, (((0,), (0,)), ((), ())), preferred_element_type=F32)


def mult(value, of):
    return pl.multiple_of(value, of)


class Links:
    def __init__(self, send, recv, early):
        self.send, self.recv, self.early, self.count = send, recv, early, 0
        self.open, self.flushed = ([], []), False

    def start(self, src, dst, peer):
        i = self.count
        self.count += 1
        group = int(getattr(src, "ref", src) is self.early and not self.flushed)
        copy = pltpu.make_async_remote_copy(
            src_ref=src,
            dst_ref=dst,
            send_sem=self.send.at[group],
            recv_sem=self.recv.at[i],
            device_id=peer,
            device_id_type=MESH,
        )
        copy.start()
        self.open[group].append(copy)
        return (i, peer)

    def arrived(self, handle, where):
        i, peer = handle
        pltpu.make_async_remote_copy(
            src_ref=where,
            dst_ref=where,
            send_sem=self.send.at[0],
            recv_sem=self.recv.at[i],
            device_id=peer,
            device_id_type=MESH,
        ).wait_recv()

    def flush(self, group):
        for copy in self.open[group]:
            copy.wait_send()
        self.flushed = True


def kernel(
    tok_in, cot_in, w1_in, w2_in,
    out_ref, ing_ref, g1_ref, g2_ref,
    w1, w2, tok, cot, tok_t, act, act_t, slope, hg, oterm, p1, p2,
    rsw1, rsw2, rza1, rza2, rzb1, rzb2,
    ra1, ra2, ra3, ra4, rb1, rb2, rb3, rb4,
    swap_in, swap_out, stage, shards, results, send, recv, local,
):
    xh, z, y, xl, c = (lax.axis_index(a) for a in AXES)
    x = xh * 2 + xl
    xp, xm = lax.rem(x + 1, 4), lax.rem(x + 3, 4)
    ph, pll = xp // 2, lax.rem(xp, 2)
    mh, ml = xm // 2, lax.rem(xm, 2)
    yp, ym, y2 = lax.rem(y + 1, 4), lax.rem(y + 3, 4), lax.rem(y + 2, 4)
    zp, zm, z2 = lax.rem(z + 1, 4), lax.rem(z + 3, 4), lax.rem(z + 2, 4)
    oc = 1 - c
    XP, XM = {"xh": ph, "xl": pll}, {"xh": mh, "xl": ml}
    YP, YM, ZP, ZM, OC = {"y": yp}, {"y": ym}, {"z": zp}, {"z": zm}, {"c": oc}
    H = B // 2
    OWN, OTHER = 0, 1
    own_h, other_h = xh, 1 - xh
    links = Links(send, recv, tok)
    start, arrived = links.start, links.arrived

    loads = [
        pltpu.make_async_copy(ref, shards.at[k], local.at[4 + k]) for k, ref in enumerate((tok_in, cot_in))
    ]
    for load in loads:
        load.start()
    bar = pltpu.get_barrier_semaphore()
    for peer in (XP, XM, YP, YM, ZP, ZM, OC):
        pl.semaphore_signal(bar, inc=1, device_id=peer, device_id_type=MESH)
    pl.semaphore_wait(bar, 7)

    def rows_a(hv, lo=0, n=RA):
        return pl.ds(mult(hv * RA + lo, 16), n)

    def rows_b(hv, lo=0, n=RB):
        return pl.ds(mult(2 * RA + hv * RB + lo, 16), n)

    def cols(yv, lv):
        return pl.ds(mult((yv * 2 + lv) * B, 128), B)

    def line(yv):
        return pl.ds(mult(yv * 2 * B, 128), 2 * B)

    def loc1(ref, hv, zv, cv, lo=0, n=B):
        return ref.at[pl.ds(mult((hv * 4 + zv) * B + lo, 64), n), pl.ds(mult(cv * B, 128), B)]

    def loc2(ref, hv, zv, cv, lo=0, n=B):
        return ref.at[pl.ds(mult(cv * B + lo, 64), n), pl.ds(mult((hv * 4 + zv) * B, 128), B)]

    def half1(ref, hv, lo=0, n=B):
        return ref.at[pl.ds(lo, n), pl.ds(mult(hv * B, 128), B)]

    def half2(ref, hv, lo=0, n=B):
        return ref.at[pl.ds(mult(hv * B + lo, 64), n), :]

    class Weights:
        def __init__(self, k, shard, ref, loc, half):
            self.at = lambda b, zv, *part: loc(ref, (own_h, other_h)[b], zv, c, *part)
            self.other = lambda b, zv: loc(ref, (own_h, other_h)[b], zv, oc)
            self.relayed = lambda hv, *part: loc(ref, hv, z, c, *part)
            self.swaps, self.z1, self.z2 = [], {}, {}
            self.k, self.shard, self.half = k, shard, half

        def swap(self, b, zv, src=None):
            block = self.at(b, zv)
            self.swaps.append((start(block if src is None else src, block, OC), b, zv))

        def exchange(self):
            self.x1 = tuple(
                start(self.half(self.shard, other_h, lo, H), stage.at[self.k, i], peer)
                for i, (lo, peer) in enumerate(((0, XP), (H, XM)))
            )

        def relay(self):
            arrived(self.x1[0], stage.at[self.k, 0])
            s0 = start(stage.at[self.k, 0], self.relayed(mh, 0, H), XP)
            arrived(self.x1[1], stage.at[self.k, 1])
            s1 = start(stage.at[self.k, 1], self.relayed(ph, H, H), XM)
            self.x2 = s0, s1

        def own(self):
            src, dst = self.half(self.shard, own_h), self.at(OWN, z)
            self.z1[OWN] = start(src, dst, ZP), start(src, dst, ZM)
            self.swap(OWN, z, src)
            self.copy = pltpu.make_async_copy(src, dst, local.at[self.k])
            self.copy.start()

        def partner(self):
            block = self.at(OTHER, z)
            arrived(self.x2[0], self.at(OTHER, z, 0, H))
            arrived(self.x2[1], self.at(OTHER, z, H, H))
            self.z1[OTHER] = start(block, block, ZP), start(block, block, ZM)
            self.swap(OTHER, z)

        def forward(self, b):
            p, m = self.z1[b]
            from_m, from_p = self.at(b, zm), self.at(b, zp)
            if b == OWN:
                arrived(p, from_m)
                self.z2[b] = start(from_m, from_m, ZP)
                arrived(m, from_p)
            else:
                arrived(m, from_p)
                self.z2[b] = start(from_p, from_p, ZM)
                arrived(p, from_m)
            self.swap(b, zm)
            self.swap(b, zp)

        def last(self, b):
            arrived(self.z2[b], self.at(b, z2))
            self.swap(b, z2)

        def whole(self):
            self.copy.wait()
            for handle, b, zv in self.swaps:
                arrived(handle, self.other(b, zv))

    xs = {"o": (xh, xl), "m": (mh, ml), "p": (ph, pll), "t": (1 - xh, xl)}
    ys = {"o": y, "m": ym, "p": yp, "t": y2}
    PLUS = "om"

    def place_a(ref, i, j, lo=0, n=RA):
        (hv, lv), yv = xs[i], ys[j]
        return ref.at[rows_a(hv, lo, n), cols(yv, lv)]

    def place_b(ref, i, j, lo=0, n=RB):
        (hv, lv), yv = xs[j], ys[i]
        return ref.at[rows_b(hv, lo, n), cols(yv, lv)]

    ROUTES = {"a": (place_a, SPLIT_A, (XP, XM), (YP, YM)), "b": (place_b, SPLIT_B, (YP, YM), (XP, XM))}

    pick_row = lax.broadcasted_iota(jnp.int32, (192, B), 0)
    pick_col = lax.broadcasted_iota(jnp.int32, (192, B), 1)
    ours = (pick_col == pick_row + 192 * c).astype(BF16)
    theirs = (pick_col == pick_row + 192 * oc).astype(BF16)

    class GatherPart:
        def __init__(self, ref, route):
            place, self.split, self.first, self.second = ROUTES[route]
            self.at = lambda *where: place(ref, *where)
            self.f2, self.s1, self.s2 = {}, {}, {}

        def both(self, i):
            block = self.at(i, "o")
            self.s1[i] = tuple(start(block, block, peer) for peer in self.second)

        def own_first(self):
            block = self.at("o", "o")
            self.f1 = tuple(start(block, block, peer) for peer in self.first)

        def near(self, i):
            n0, n1 = self.split
            p, m = self.first
            if i == "m":
                arrived(self.f1[0], self.at("m", "o"))
                block = self.at("m", "o", 0, n0)
                self.f2[0] = start(block, block, p)
            else:
                arrived(self.f1[1], self.at("p", "o"))
                block = self.at("p", "o", n0, n1)
                self.f2[1] = start(block, block, m)
            self.both(i)

        def far(self):
            n0, n1 = self.split
            arrived(self.f2[0], self.at("t", "o", 0, n0))
            arrived(self.f2[1], self.at("t", "o", n0, n1))
            self.both("t")

        def forward(self, i):
            from_m, from_p = self.at(i, "m"), self.at(i, "p")
            if i in PLUS:
                arrived(self.s1[i][0], from_m)
                self.s2[i] = start(from_m, from_m, self.second[0])
                arrived(self.s1[i][1], from_p)
            else:
                arrived(self.s1[i][1], from_p)
                self.s2[i] = start(from_p, from_p, self.second[1])
                arrived(self.s1[i][0], from_m)

        def whole(self):
            for i in "ompt":
                arrived(self.s2[i], self.at(i, "t"))

    class Gather:
        def __init__(self, shard, ref, k):
            self.ref, self.shard, self.k = ref, shard, k
            self.a, self.b = GatherPart(ref, "a"), GatherPart(ref, "b")

        def swap(self):
            src = self.shard.at[:, pl.ds(mult(oc * HALF, HALF), HALF)]
            self.swapped = start(src, swap_in.at[self.k], OC)

        def assemble(self):
            arrived(self.swapped, swap_in.at[self.k])
            loads[self.k].wait()
            mine = shards[self.k, :, pl.ds(mult(c * HALF, HALF), HALF)]
            block = (dot_tn(mine, ours) + dot_tn(swap_in[self.k], theirs)).astype(BF16)
            self.ref[rows_a(xh), cols(y, xl)] = block[:RA]
            self.ref[rows_b(xh), cols(y, xl)] = block[RA:]

        def whole(self):
            self.a.whole()
            self.b.whole()

        def flush(self):
            links.flush(1)

    def add_into(where, *parts):
        total = where[...].astype(F32)
        for part in parts:
            total = total + part.astype(F32)
        where[...] = total.astype(BF16)

    class SumPart:
        def __init__(self, ref, route, k, r1, r2, r3, r4):
            place, self.split, self.first, self.second = ROUTES[route]
            self.at = lambda *where: place(ref, *where)
            self.r1, self.r2, self.r3, self.r4 = r1.at[k], r2.at[k], r3.at[k], r4.at[k]
            self.s0, self.s1, self.s2, self.s4 = {}, {}, {}, {}

        def far(self, i):
            n = "ompt".index(i)
            peer = self.second[0] if i in PLUS else self.second[1]
            self.s1[i] = start(self.at(i, "t"), self.r1.at[n], peer)

        def early(self, i):
            n = "ompt".index(i)
            if i in PLUS:
                self.s0[i] = start(self.at(i, "m"), self.r2.at[1, n], self.second[1])
            else:
                self.s0[i] = start(self.at(i, "p"), self.r2.at[0, n], self.second[0])

        def near(self, i):
            n = "ompt".index(i)
            arrived(self.s1[i], self.r1.at[n])
            if i in PLUS:
                add_into(self.at(i, "p"), self.r1[n])
                p = start(self.at(i, "p"), self.r2.at[0, n], self.second[0])
                self.s2[i] = p, self.s0[i]
            else:
                add_into(self.at(i, "m"), self.r1[n])
                m = start(self.at(i, "m"), self.r2.at[1, n], self.second[1])
                self.s2[i] = self.s0[i], m

        def summed(self, i, wait=True):
            n = "ompt".index(i)
            if wait:
                arrived(self.s2[i][0], self.r2.at[0, n])
                arrived(self.s2[i][1], self.r2.at[1, n])
            return self.r2[0, n], self.r2[1, n]

        def first_far(self):
            add_into(self.at("t", "o"), *self.summed("t"))
            n0, n1 = self.split
            self.s3 = (
                start(self.at("t", "o", 0, n0), self.r3.at[0, pl.ds(0, n0)], self.first[0]),
                start(self.at("t", "o", n0, n1), self.r3.at[1, pl.ds(0, n1)], self.first[1]),
            )

        def first_near(self, i):
            n0, n1 = self.split
            if i == "p":
                arrived(self.s3[0], self.r3.at[0, pl.ds(0, n0)])
                add_into(self.at("p", "o", n0, n1), *(r[n0:] for r in self.summed("p")))
                add_into(self.at("p", "o", 0, n0), self.r3[0, :n0], *(r[:n0] for r in self.summed("p", False)))
                self.s4[0] = start(self.at("p", "o"), self.r4.at[0], self.first[0])
            else:
                arrived(self.s3[1], self.r3.at[1, pl.ds(0, n1)])
                add_into(self.at("m", "o", 0, n0), *(r[:n0] for r in self.summed("m")))
                add_into(self.at("m", "o", n0, n1), self.r3[1, :n1], *(r[n0:] for r in self.summed("m", False)))
                self.s4[1] = start(self.at("m", "o"), self.r4.at[1], self.first[1])

        def total(self):
            parts = self.summed("o")
            arrived(self.s4[0], self.r4.at[0])
            arrived(self.s4[1], self.r4.at[1])
            value = self.at("o", "o")[...].astype(F32)
            for part in (*parts, self.r4[0], self.r4[1]):
                value = value + part.astype(F32)
            return value.astype(BF16)

    class Plane:
        def __init__(self, ref, k, result):
            self.k, self.result = k, result
            self.a = SumPart(ref, "a", k, ra1, ra2, ra3, ra4)
            self.b = SumPart(ref, "b", k, rb1, rb2, rb3, rb4)

        def done(self):
            k = self.k
            total = jnp.concatenate([self.a.total(), self.b.total()], axis=0)
            mine = pl.ds(mult(c * HALF, HALF), HALF)
            swap_out[k] = dot_nt(theirs, total).astype(BF16)
            self.last = start(swap_out.at[k], self.result.at[:, mine], OC)
            results[k] = dot_nt(ours, total).astype(BF16)
            self.copy = pltpu.make_async_copy(results.at[k], self.result.at[:, mine], local.at[6 + k])
            self.copy.start()

        def whole(self):
            self.copy.wait()
            arrived(self.last, self.result.at[:, pl.ds(mult(oc * HALF, HALF), HALF)])

    class Grad:
        def __init__(self, k, ref, loc, rsw, rz1, rz2, result, half):
            self.at = lambda b, zv, *part: loc(ref, (own_h, other_h)[b], zv, c, *part)
            self.theirs = lambda b, zv: loc(ref, (own_h, other_h)[b], zv, oc)
            self.k, self.rsw, self.rz1, self.rz2, self.result, self.half = k, rsw, rz1, rz2, result, half
            self.swaps, self.s0, self.s1, self.s2 = {}, {}, {}, {}

        def swap(self, j, zv):
            for b in (OTHER, OWN):
                self.swaps[j, b] = start(self.theirs(b, zv), self.rsw.at[j, b], OC)

        def swapped(self, j, zv, b):
            arrived(self.swaps[j, b], self.rsw.at[j, b])
            add_into(self.at(b, zv), self.rsw[j, b])

        def far(self, b):
            self.s1[b] = start(self.at(b, z2), self.rz1.at[b], ZP if b == OWN else ZM)

        def early(self, b):
            if b == OWN:
                self.swapped(2, zm, b)
                self.s0[b] = start(self.at(b, zm), self.rz2.at[1, b], ZM)
            else:
                self.swapped(1, zp, b)
                self.s0[b] = start(self.at(b, zp), self.rz2.at[0, b], ZP)

        def near(self, b):
            arrived(self.s1[b], self.rz1.at[b])
            j, zv = (1, zp) if b == OWN else (2, zm)
            arrived(self.swaps[j, b], self.rsw.at[j, b])
            add_into(self.at(b, zv), self.rsw[j, b], self.rz1[b])
            if b == OWN:
                self.s2[b] = start(self.at(b, zp), self.rz2.at[0, b], ZP), self.s0[b]
            else:
                self.s2[b] = self.s0[b], start(self.at(b, zm), self.rz2.at[1, b], ZM)

        def total(self, b):
            arrived(self.s2[b][0], self.rz2.at[0, b])
            arrived(self.s2[b][1], self.rz2.at[1, b])
            arrived(self.swaps[3, b], self.rsw.at[3, b])
            add_into(self.at(b, z), self.rsw[3, b], self.rz2[0, b], self.rz2[1, b])
            if b == OWN:
                self.copy = pltpu.make_async_copy(
                    self.at(b, z), self.half(self.result, own_h), local.at[self.k]
                )
                self.copy.start()
            else:
                self.s3 = tuple(
                    start(self.at(b, z, lo, H), stage.at[self.k, i], peer)
                    for i, (lo, peer) in enumerate(((0, XP), (H, XM)))
                )

        def relay(self):
            arrived(self.s3[0], stage.at[self.k, 0])
            s0 = start(stage.at[self.k, 0], self.half(self.result, mh, 0, H), XP)
            arrived(self.s3[1], stage.at[self.k, 1])
            s1 = start(stage.at[self.k, 1], self.half(self.result, ph, H, H), XM)
            self.s4 = s0, s1

        def whole(self):
            self.copy.wait()
            arrived(self.s4[0], self.half(self.result, other_h, 0, H))
            arrived(self.s4[1], self.half(self.result, other_h, H, H))

    def transpose_tokens():
        @pl.loop(0, D // 256)
        def _(j):
            at = pl.ds(mult(j * 256, 256), 256)
            tok_t[at, :] = tok[:, at].T

    def hidden(j):
        at = pl.ds(j * 256, 256)
        for lo in range(0, TOK, 256):
            rows = pl.ds(lo, 256)
            pre = dot(tok[rows, :], w1[:, at])
            cdf = 0.5 * (1.0 + lax.erf(pre * inv_root_two))
            value = (pre * cdf).astype(BF16)
            act[rows, at] = value
            act_t[at, rows] = value.T
            slope[rows, at] = cdf + pre * jnp.exp(-0.5 * pre * pre) * inv_root_tau

    def output_terms(yv):
        oterm[:, line(yv)] = dot(act[...], w2[:, line(yv)]).astype(BF16)

    def second_terms(zv):
        for hv in range(2):
            at = pl.ds(mult((hv * 4 + zv) * B, 128), B)
            p2[:, at] = dot(act_t[...], cot[:, at]).astype(BF16)

    def hidden_grad(j):
        at = pl.ds(j * 256, 256)
        for lo in range(0, TOK, 256):
            rows = pl.ds(lo, 256)
            back = dot_nt(cot[rows, :], w2[at, :])
            hg[rows, at] = (back * slope[rows, at]).astype(BF16)

    def first_terms(zv):
        for hv in range(2):
            at = pl.ds(mult((hv * 4 + zv) * B, 128), B)
            p1[at, :] = dot(tok_t[at, :], hg[...]).astype(BF16)

    def input_terms(yv):
        tok[:, line(yv)] = dot_nt(hg[...], w1[line(yv), :]).astype(BF16)

    wf = Weights(0, w1_in, w1, loc1, half1)
    ws = Weights(1, w2_in, w2, loc2, half2)
    gt = Gather(tok_in, tok, 0)
    gc = Gather(cot_in, cot, 1)
    po = Plane(oterm, 0, out_ref)
    pi = Plane(tok, 1, ing_ref)
    gs = Grad(2, p2, loc2, rsw2, rza2, rzb2, g2_ref, half2)
    gf = Grad(3, p1, loc1, rsw1, rza1, rzb1, g1_ref, half1)
    gt.swap()
    wf.exchange()
    wf.own()
    gc.swap()
    gt.assemble()
    gt.b.own_first()
    gc.assemble()
    gt.a.own_first()
    ws.own()
    gt.a.both("o")
    gc.b.own_first()
    wf.relay()
    gc.a.both("o")
    ws.exchange()
    wf.forward(OWN)
    gt.a.forward("o")
    gc.b.near("p")
    wf.partner()
    gt.a.near("p")
    gt.a.near("m")
    ws.relay()
    gc.a.own_first()
    gt.b.near("p")
    gc.b.both("o")
    gt.b.near("m")
    gt.b.both("o")
    gc.b.near("m")
    gt.a.far()
    ws.partner()
    gt.a.forward("p")
    ws.forward(OWN)
    wf.last(OWN)
    gt.a.forward("m")
    gc.a.near("m")
    gc.b.far()
    gc.a.near("p")
    gt.b.far()
    gt.a.forward("t")
    wf.forward(OTHER)
    gt.b.forward("p")
    gc.a.far()
    gc.b.forward("p")
    gc.a.forward("o")
    gt.b.forward("o")
    gt.b.forward("m")
    ws.forward(OTHER)
    gc.a.forward("m")
    gt.b.forward("t")
    gc.a.forward("p")
    gc.b.forward("m")
    wf.last(OTHER)
    gc.b.forward("t")
    gt.whole()
    gc.a.forward("t")
    wf.whole()
    gc.b.forward("o")
    hidden(0)
    hidden(2)
    hidden(1)
    ws.last(OWN)
    ws.last(OTHER)
    transpose_tokens()
    gc.whole()
    second_terms(z2)
    gs.swap(0, z2)
    ws.whole()
    output_terms(y2)
    po.a.far("t")
    po.a.far("m")
    po.b.early("t")
    output_terms(ym)
    output_terms(yp)
    gt.flush()
    po.a.far("p")
    po.b.far("m")
    gs.swapped(0, z2, OWN)
    po.b.far("t")
    po.b.far("p")
    gs.swapped(0, z2, OTHER)
    gs.far(OTHER)
    gs.far(OWN)
    hidden_grad(1)
    po.a.early("t")
    hidden_grad(2)
    hidden_grad(0)
    first_terms(z2)
    gf.swap(0, z2)
    po.b.early("m")
    po.b.early("p")
    po.a.near("t")
    po.a.early("p")
    po.a.early("m")
    input_terms(yp)
    po.b.near("m")
    pi.a.early("t")
    po.b.near("p")
    input_terms(y2)
    po.a.near("p")
    gf.swapped(0, z2, OTHER)
    pi.a.far("t")
    pi.b.far("t")
    po.a.near("m")
    gf.far(OTHER)
    pi.a.early("p")
    pi.a.far("p")
    pi.b.early("t")
    gf.swapped(0, z2, OWN)
    gf.far(OWN)
    pi.b.early("p")
    po.b.near("t")
    second_terms(zp)
    gs.swap(1, zp)
    po.a.far("o")
    output_terms(y)
    po.a.first_far()
    second_terms(zm)
    pi.a.far("m")
    pi.b.far("p")
    po.b.far("o")
    pi.b.near("t")
    gs.swap(2, zm)
    input_terms(ym)
    first_terms(zp)
    pi.b.far("m")
    gs.early(OTHER)
    pi.b.early("m")
    po.b.early("o")
    gf.swap(1, zp)
    input_terms(y)
    pi.b.far("o")
    gs.near(OTHER)
    first_terms(z)
    pi.b.near("p")
    gf.swap(3, z)
    po.b.near("o")
    po.b.first_far()
    pi.b.early("o")
    second_terms(z)
    pi.b.near("m")
    po.a.first_near("p")
    pi.b.first_far()
    first_terms(zm)
    gf.early(OTHER)
    gf.swap(2, zm)
    pi.a.near("t")
    gs.swap(3, z)
    po.a.first_near("m")
    gf.near(OTHER)
    pi.b.near("o")
    pi.a.early("m")
    pi.a.near("p")
    gf.early(OWN)
    gs.total(OTHER)
    pi.a.far("o")
    gf.near(OWN)
    pi.b.first_near("m")
    pi.a.first_far()
    pi.a.near("m")
    gs.early(OWN)
    gs.near(OWN)
    pi.a.early("o")
    pi.b.first_near("p")
    po.b.first_near("p")
    po.a.early("o")
    gs.relay()
    po.a.near("o")
    gf.total(OTHER)
    pi.a.first_near("p")
    pi.a.first_near("m")
    pi.a.near("o")
    po.b.first_near("m")
    gf.relay()
    po.done()
    gf.total(OWN)
    pi.done()
    gs.total(OWN)
    for part in (po, gs, gf, pi):
        part.whole()
    links.flush(0)


def widen(out_in, ing_in, g1_in, g2_in, out_ref, ing_ref, g1_ref, g2_ref):
    out_ref[...] = out_in[...]
    ing_ref[...] = ing_in[...]
    g1_ref[...] = g1_in[...].astype(F32)
    g2_ref[...] = g2_in[...].astype(F32)


def shards(tokens, w_first, w_second, cotangent):
    hbm = pl.BlockSpec(memory_space=pl.ANY)
    parts = pl.pallas_call(
        kernel,
        name="mlp",
        out_shape=(
            jax.ShapeDtypeStruct((192, TOK), BF16),
            jax.ShapeDtypeStruct((192, TOK), BF16),
            jax.ShapeDtypeStruct((B, 2 * B), BF16),
            jax.ShapeDtypeStruct((2 * B, B), BF16),
        ),
        in_specs=[hbm] * 4,
        out_specs=(hbm,) * 4,
        scratch_shapes=[
            pltpu.VMEM((D, HID), BF16),
            pltpu.VMEM((HID, D), BF16),
            pltpu.VMEM((TOK, D), BF16),
            pltpu.VMEM((TOK, D), BF16),
            pltpu.VMEM((D, TOK), BF16),
            pltpu.VMEM((TOK, HID), BF16),
            pltpu.VMEM((HID, TOK), BF16),
            pltpu.VMEM((TOK, HID), F32),
            pltpu.VMEM((TOK, HID), BF16),
            pltpu.VMEM((TOK, D), BF16),
            pltpu.VMEM((D, HID), BF16),
            pltpu.VMEM((HID, D), BF16),
            pltpu.VMEM((4, 2, B, B), BF16),
            pltpu.VMEM((4, 2, B, B), BF16),
            pltpu.VMEM((2, B, B), BF16),
            pltpu.VMEM((2, B, B), BF16),
            pltpu.VMEM((2, 2, B, B), BF16),
            pltpu.VMEM((2, 2, B, B), BF16),
            pltpu.VMEM((2, 4, RA, B), BF16),
            pltpu.VMEM((2, 2, 4, RA, B), BF16),
            pltpu.VMEM((2, 2, SPLIT_A[0], B), BF16),
            pltpu.VMEM((2, 2, RA, B), BF16),
            pltpu.VMEM((2, 4, RB, B), BF16),
            pltpu.VMEM((2, 2, 4, RB, B), BF16),
            pltpu.VMEM((2, 2, SPLIT_B[0], B), BF16),
            pltpu.VMEM((2, 2, RB, B), BF16),
            pltpu.VMEM((2, 192, HALF), BF16),
            pltpu.VMEM((2, 192, HALF), BF16),
            pltpu.VMEM((4, 2, B // 2, B), BF16),
            pltpu.VMEM((2, 192, TOK), BF16),
            pltpu.VMEM((2, 192, HALF), BF16),
            pltpu.SemaphoreType.DMA((2,)),
            pltpu.SemaphoreType.DMA((NSEM,)),
            pltpu.SemaphoreType.DMA((8,)),
        ],
        compiler_params=pltpu.CompilerParams(
            collective_id=0, has_side_effects=True, vmem_limit_bytes=60 * 1024 * 1024
        ),
        cost_estimate=pl.CostEstimate(flops=14_500_000_000, bytes_accessed=40_000_000, transcendentals=800_000),
    )(tokens.T, cotangent.T, w_first, w_second)
    steps = 3
    specs = [pl.BlockSpec((part.shape[0] // steps, part.shape[1]), lambda i: (i, 0)) for part in parts]
    outputs, input_grad, first_grad, second_grad = pl.pallas_call(
        widen,
        name="widen",
        grid=(steps,),
        out_shape=[
            jax.ShapeDtypeStruct(part.shape, dtype) for part, dtype in zip(parts, (BF16, BF16, F32, F32))
        ],
        in_specs=specs,
        out_specs=specs,
    )(*parts)
    return outputs.T, input_grad.T, first_grad, second_grad


def solution(mesh):
    finer = Mesh(mesh.devices.reshape(2, 4, 4, 2, 2), AXES)
    in_specs = (P(DP, MP), P(DP, MP), P(MP, DP), P(DP, MP))
    out_specs = (P(DP, MP), P(DP, MP), P(DP, MP), P(MP, DP))
    return jax.shard_map(
        shards, mesh=finer, in_specs=in_specs, out_specs=out_specs, check_vma=False
    )
```

```python
import jax
import jax.numpy as jnp
from jax import lax
from jax.experimental import pallas as pl
from jax.experimental.pallas import tpu as pltpu
from jax.sharding import Mesh
from jax.sharding import PartitionSpec as P

AXES = ("xh", "z", "y", "xl", "c")
DP = ("xh", "z")
MP = ("y", "xl", "c")
MESH = pl.DeviceIdType.MESH
F32 = jnp.float32
BF16 = jnp.bfloat16

D = 3072
B = 384
HID = 768
TOK = 512
HALF = 256
RA = 176
RB = HALF - RA
SPLIT_A = (96, 80)
SPLIT_B = (48, 32)
NSEM = 156

inv_root_two = 0.7071067811865476
inv_root_tau = 0.3989422804014327


def dot(a, b):
    return jnp.dot(a, b, preferred_element_type=F32)


def dot_nt(a, b):
    return lax.dot_general(a, b, (((1,), (1,)), ((), ())), preferred_element_type=F32)


def dot_tn(a, b):
    return lax.dot_general(a, b, (((0,), (0,)), ((), ())), preferred_element_type=F32)


def mult(value, of):
    return pl.multiple_of(value, of)


class Links:
    def __init__(self, send, recv, early):
        self.send, self.recv, self.early, self.count = send, recv, early, 0
        self.open, self.flushed = ([], []), False
        self.sems, self.shared = 0, {}

    def start(self, src, dst, peer, *share):
        i = self.count
        self.count += 1
        sem = self.shared.get(share, self.sems)
        if sem == self.sems:
            self.sems += 1
        if share:
            self.shared[share] = sem
        group = int(getattr(src, "ref", src) is self.early and not self.flushed)
        copy = pltpu.make_async_remote_copy(
            src_ref=src,
            dst_ref=dst,
            send_sem=self.send.at[group],
            recv_sem=self.recv.at[sem],
            device_id=peer,
            device_id_type=MESH,
        )
        copy.start()
        self.open[group].append(copy)
        return i, peer, sem

    def arrived(self, handle, where):
        i, peer, sem = handle
        pltpu.make_async_remote_copy(
            src_ref=where,
            dst_ref=where,
            send_sem=self.send.at[0],
            recv_sem=self.recv.at[sem],
            device_id=peer,
            device_id_type=MESH,
        ).wait_recv()

    def flush(self, group):
        for copy in self.open[group]:
            copy.wait_send()
        self.flushed = True


def kernel(
    tok_in, cot_in, w1_in, w2_in,
    out_ref, ing_ref, g1_ref, g2_ref,
    w1, w2, tok, cot, tok_t, act, act_t, slope, hg, oterm, p1, p2,
    rsw1, rsw2, rza1, rza2, rzb1, rzb2,
    ra1, ra2, ra3, ra4, rb1, rb2, rb3, rb4,
    swap_in, swap_out, stage, shards, results, send, recv, local,
):
    xh, z, y, xl, c = (lax.axis_index(a) for a in AXES)
    x = xh * 2 + xl
    xp, xm = lax.rem(x + 1, 4), lax.rem(x + 3, 4)
    ph, pll = xp // 2, lax.rem(xp, 2)
    mh, ml = xm // 2, lax.rem(xm, 2)
    yp, ym, y2 = lax.rem(y + 1, 4), lax.rem(y + 3, 4), lax.rem(y + 2, 4)
    zp, zm, z2 = lax.rem(z + 1, 4), lax.rem(z + 3, 4), lax.rem(z + 2, 4)
    oc = 1 - c
    XP, XM = {"xh": ph, "xl": pll}, {"xh": mh, "xl": ml}
    YP, YM, ZP, ZM, OC = {"y": yp}, {"y": ym}, {"z": zp}, {"z": zm}, {"c": oc}
    H = B // 2
    OWN, OTHER = 0, 1
    own_h, other_h = xh, 1 - xh
    links = Links(send, recv, tok)
    start, arrived = links.start, links.arrived

    loads = [
        pltpu.make_async_copy(ref, shards.at[k], local.at[4 + k]) for k, ref in enumerate((tok_in, cot_in))
    ]
    for load in loads:
        load.start()
    bar = pltpu.get_barrier_semaphore()
    for peer in (XP, XM, YP, YM, ZP, ZM, OC):
        pl.semaphore_signal(bar, inc=1, device_id=peer, device_id_type=MESH)
    pl.semaphore_wait(bar, 7)

    def rows_a(hv, lo=0, n=RA):
        return pl.ds(mult(hv * RA + lo, 16), n)

    def rows_b(hv, lo=0, n=RB):
        return pl.ds(mult(2 * RA + hv * RB + lo, 16), n)

    def cols(yv, lv):
        return pl.ds(mult((yv * 2 + lv) * B, 128), B)

    def line(yv):
        return pl.ds(mult(yv * 2 * B, 128), 2 * B)

    def loc1(ref, hv, zv, cv, lo=0, n=B):
        return ref.at[pl.ds(mult((hv * 4 + zv) * B + lo, 64), n), pl.ds(mult(cv * B, 128), B)]

    def loc2(ref, hv, zv, cv, lo=0, n=B):
        return ref.at[pl.ds(mult(cv * B + lo, 64), n), pl.ds(mult((hv * 4 + zv) * B, 128), B)]

    def half1(ref, hv, lo=0, n=B):
        return ref.at[pl.ds(lo, n), pl.ds(mult(hv * B, 128), B)]

    def half2(ref, hv, lo=0, n=B):
        return ref.at[pl.ds(mult(hv * B + lo, 64), n), :]

    class Weights:
        def __init__(self, k, shard, ref, loc, half, theirs):
            self.at = lambda b, zv, *part: loc(ref, (own_h, other_h)[b], zv, c, *part)
            self.theirs = theirs
            self.relayed = lambda hv, *part: loc(ref, hv, z, c, *part)
            self.swaps, self.z1, self.z2 = [], {}, {}
            self.k, self.shard, self.half = k, shard, half

        def swap(self, b, zv, src=None):
            block = self.at(b, zv)
            self.swaps.append(start(block if src is None else src, block, OC, "w", self.k))

        def exchange(self):
            self.x1 = tuple(
                start(self.half(self.shard, other_h, lo, H), stage.at[self.k, i], peer)
                for i, (lo, peer) in enumerate(((0, XP), (H, XM)))
            )

        def relay(self):
            arrived(self.x1[0], stage.at[self.k, 0])
            s0 = start(stage.at[self.k, 0], self.relayed(mh, 0, H), XP, "x", self.k)
            arrived(self.x1[1], stage.at[self.k, 1])
            s1 = start(stage.at[self.k, 1], self.relayed(ph, H, H), XM, "x", self.k)
            self.x2 = s0, s1

        def own(self):
            src, dst = self.half(self.shard, own_h), self.at(OWN, z)
            self.z1[OWN] = start(src, dst, ZP), start(src, dst, ZM)
            self.swap(OWN, z, src)
            self.copy = pltpu.make_async_copy(src, dst, local.at[self.k])
            self.copy.start()

        def partner(self):
            block = self.at(OTHER, z)
            arrived(self.x2[0], block)
            self.z1[OTHER] = start(block, block, ZP), start(block, block, ZM)
            self.swap(OTHER, z)

        def forward(self, b):
            p, m = self.z1[b]
            from_m, from_p = self.at(b, zm), self.at(b, zp)
            if b == OWN:
                arrived(p, from_m)
                self.z2[b] = start(from_m, from_m, ZP)
                arrived(m, from_p)
            else:
                arrived(m, from_p)
                self.z2[b] = start(from_p, from_p, ZM)
                arrived(p, from_m)
            self.swap(b, zm)
            self.swap(b, zp)

        def last(self, b):
            arrived(self.z2[b], self.at(b, z2))
            self.swap(b, z2)

        def whole(self):
            self.copy.wait()
            arrived(self.swaps[0], self.theirs)

    xs = {"o": (xh, xl), "m": (mh, ml), "p": (ph, pll), "t": (1 - xh, xl)}
    ys = {"o": y, "m": ym, "p": yp, "t": y2}
    PLUS = "om"

    def place_a(ref, i, j, lo=0, n=RA):
        (hv, lv), yv = xs[i], ys[j]
        return ref.at[rows_a(hv, lo, n), cols(yv, lv)]

    def place_b(ref, i, j, lo=0, n=RB):
        (hv, lv), yv = xs[j], ys[i]
        return ref.at[rows_b(hv, lo, n), cols(yv, lv)]

    ROUTES = {"a": (place_a, SPLIT_A, (XP, XM), (YP, YM)), "b": (place_b, SPLIT_B, (YP, YM), (XP, XM))}

    pick_row = lax.broadcasted_iota(jnp.int32, (192, B), 0)
    pick_col = lax.broadcasted_iota(jnp.int32, (192, B), 1)
    ours = (pick_col == pick_row + 192 * c).astype(BF16)
    theirs = (pick_col == pick_row + 192 * oc).astype(BF16)

    class GatherPart:
        def __init__(self, ref, route, k):
            self.route, self.k, self.key = route, k, ("g", k) if route == "a" else ()
            self.far_line = ref.at[pl.ds(0, 2 * RA), line(y2)]
            place, self.split, self.first, self.second = ROUTES[route]
            self.at = lambda *where: place(ref, *where)
            self.f2, self.s1, self.s2 = {}, {}, {}

        def both(self, i):
            block = self.at(i, "o")
            self.s1[i] = tuple(start(block, block, peer) for peer in self.second)

        def own_first(self):
            block = self.at("o", "o")
            self.f1 = tuple(start(block, block, peer) for peer in self.first)

        def near(self, i):
            n0, n1 = self.split
            p, m = self.first
            if i == "m":
                arrived(self.f1[0], self.at("m", "o"))
                block = self.at("m", "o", 0, n0)
                self.f2[0] = start(block, block, p, "f", self.route, self.k)
            else:
                arrived(self.f1[1], self.at("p", "o"))
                block = self.at("p", "o", n0, n1)
                self.f2[1] = start(block, block, m, "f", self.route, self.k)
            self.both(i)

        def far(self):
            arrived(self.f2[0], self.at("t", "o"))
            self.both("t")

        def forward(self, i):
            from_m, from_p = self.at(i, "m"), self.at(i, "p")
            if i in PLUS:
                arrived(self.s1[i][0], from_m)
                self.s2[i] = start(from_m, from_m, self.second[0], *self.key)
                arrived(self.s1[i][1], from_p)
            else:
                arrived(self.s1[i][1], from_p)
                self.s2[i] = start(from_p, from_p, self.second[1], *self.key)
                arrived(self.s1[i][0], from_m)

        def whole(self):
            if self.key:
                arrived(self.s2["o"], self.far_line)
            else:
                for i in "ompt":
                    arrived(self.s2[i], self.at(i, "t"))

    class Gather:
        def __init__(self, shard, ref, k):
            self.ref, self.shard, self.k = ref, shard, k
            self.a, self.b = GatherPart(ref, "a", k), GatherPart(ref, "b", k)

        def swap(self):
            src = self.shard.at[:, pl.ds(mult(oc * HALF, HALF), HALF)]
            self.swapped = start(src, swap_in.at[self.k], OC)

        def assemble(self):
            arrived(self.swapped, swap_in.at[self.k])
            loads[self.k].wait()
            mine = shards[self.k, :, pl.ds(mult(c * HALF, HALF), HALF)]
            block = (dot_tn(mine, ours) + dot_tn(swap_in[self.k], theirs)).astype(BF16)
            self.ref[rows_a(xh), cols(y, xl)] = block[:RA]
            self.ref[rows_b(xh), cols(y, xl)] = block[RA:]

        def whole(self):
            self.a.whole()
            self.b.whole()

        def flush(self):
            links.flush(1)

    def add_into(where, *parts):
        total = where[...].astype(F32)
        for part in parts:
            total = total + part.astype(F32)
        where[...] = total.astype(BF16)

    class SumPart:
        def __init__(self, ref, route, k, r1, r2, r3, r4):
            place, self.split, self.first, self.second = ROUTES[route]
            self.at = lambda *where: place(ref, *where)
            self.key = "s", route, k
            self.r1, self.r2, self.r3, self.r4 = r1.at[k], r2.at[k], r3.at[k], r4.at[k]
            self.s0, self.s1, self.s2, self.s4 = {}, {}, {}, {}

        def far(self, i):
            n = "ompt".index(i)
            peer = self.second[0] if i in PLUS else self.second[1]
            self.s1[i] = start(self.at(i, "t"), self.r1.at[n], peer)

        def early(self, i):
            n = "ompt".index(i)
            if i in PLUS:
                self.s0[i] = start(self.at(i, "m"), self.r2.at[1, n], self.second[1], *self.key, i)
            else:
                self.s0[i] = start(self.at(i, "p"), self.r2.at[0, n], self.second[0], *self.key, i)

        def near(self, i):
            n = "ompt".index(i)
            arrived(self.s1[i], self.r1.at[n])
            if i in PLUS:
                add_into(self.at(i, "p"), self.r1[n])
                p = start(self.at(i, "p"), self.r2.at[0, n], self.second[0], *self.key, i)
                self.s2[i] = p, self.s0[i]
            else:
                add_into(self.at(i, "m"), self.r1[n])
                m = start(self.at(i, "m"), self.r2.at[1, n], self.second[1], *self.key, i)
                self.s2[i] = self.s0[i], m

        def summed(self, i, wait=True):
            n = "ompt".index(i)
            if wait:
                arrived(self.s2[i][0], self.r2.at[:, n])
            return self.r2[0, n], self.r2[1, n]

        def first_far(self):
            add_into(self.at("t", "o"), *self.summed("t"))
            n0, n1 = self.split
            self.s3 = (
                start(self.at("t", "o", 0, n0), self.r3.at[0, pl.ds(0, n0)], self.first[0]),
                start(self.at("t", "o", n0, n1), self.r3.at[1, pl.ds(0, n1)], self.first[1]),
            )

        def first_near(self, i):
            n0, n1 = self.split
            if i == "p":
                arrived(self.s3[0], self.r3.at[0, pl.ds(0, n0)])
                add_into(self.at("p", "o", n0, n1), *(r[n0:] for r in self.summed("p")))
                add_into(self.at("p", "o", 0, n0), self.r3[0, :n0], *(r[:n0] for r in self.summed("p", False)))
                self.s4[0] = start(self.at("p", "o"), self.r4.at[0], self.first[0])
            else:
                arrived(self.s3[1], self.r3.at[1, pl.ds(0, n1)])
                add_into(self.at("m", "o", 0, n0), *(r[:n0] for r in self.summed("m")))
                add_into(self.at("m", "o", n0, n1), self.r3[1, :n1], *(r[n0:] for r in self.summed("m", False)))
                self.s4[1] = start(self.at("m", "o"), self.r4.at[1], self.first[1])

        def total(self):
            parts = self.summed("o")
            arrived(self.s4[0], self.r4.at[0])
            arrived(self.s4[1], self.r4.at[1])
            value = self.at("o", "o")[...].astype(F32)
            for part in (*parts, self.r4[0], self.r4[1]):
                value = value + part.astype(F32)
            return value.astype(BF16)

    class Plane:
        def __init__(self, ref, k, result):
            self.k, self.result = k, result
            self.a = SumPart(ref, "a", k, ra1, ra2, ra3, ra4)
            self.b = SumPart(ref, "b", k, rb1, rb2, rb3, rb4)

        def done(self):
            k = self.k
            total = jnp.concatenate([self.a.total(), self.b.total()], axis=0)
            mine = pl.ds(mult(c * HALF, HALF), HALF)
            swap_out[k] = dot_nt(theirs, total).astype(BF16)
            self.last = start(swap_out.at[k], self.result.at[:, mine], OC)
            results[k] = dot_nt(ours, total).astype(BF16)
            self.copy = pltpu.make_async_copy(results.at[k], self.result.at[:, mine], local.at[6 + k])
            self.copy.start()

        def whole(self):
            self.copy.wait()
            arrived(self.last, self.result.at[:, pl.ds(mult(oc * HALF, HALF), HALF)])

    class Grad:
        def __init__(self, k, ref, loc, rsw, rz1, rz2, result, half):
            self.at = lambda b, zv, *part: loc(ref, (own_h, other_h)[b], zv, c, *part)
            self.theirs = lambda b, zv: loc(ref, (own_h, other_h)[b], zv, oc)
            self.k, self.rsw, self.rz1, self.rz2, self.result, self.half = k, rsw, rz1, rz2, result, half
            self.swaps, self.s0, self.s1, self.s2 = {}, {}, {}, {}

        def swap(self, j, zv, b):
            self.swaps[j, b] = start(self.theirs(b, zv), self.rsw.at[j, b], OC)

        def swapped(self, j, zv, b):
            arrived(self.swaps[j, b], self.rsw.at[j, b])
            add_into(self.at(b, zv), self.rsw[j, b])

        def far(self, b):
            self.s1[b] = start(self.at(b, z2), self.rz1.at[b], ZP if b == OWN else ZM)

        def early(self, b):
            if b == OWN:
                self.swapped(2, zm, b)
                self.s0[b] = start(self.at(b, zm), self.rz2.at[1, b], ZM, "t", self.k, b)
            else:
                self.swapped(1, zp, b)
                self.s0[b] = start(self.at(b, zp), self.rz2.at[0, b], ZP, "t", self.k, b)

        def near(self, b):
            arrived(self.s1[b], self.rz1.at[b])
            j, zv = (1, zp) if b == OWN else (2, zm)
            arrived(self.swaps[j, b], self.rsw.at[j, b])
            add_into(self.at(b, zv), self.rsw[j, b], self.rz1[b])
            if b == OWN:
                self.s2[b] = start(self.at(b, zp), self.rz2.at[0, b], ZP, "t", self.k, b), self.s0[b]
            else:
                self.s2[b] = self.s0[b], start(self.at(b, zm), self.rz2.at[1, b], ZM, "t", self.k, b)

        def total(self, b):
            arrived(self.s2[b][0], self.rz2.at[:, b])
            arrived(self.swaps[3, b], self.rsw.at[3, b])
            add_into(self.at(b, z), self.rsw[3, b], self.rz2[0, b], self.rz2[1, b])
            if b == OWN:
                self.copy = pltpu.make_async_copy(
                    self.at(b, z), self.half(self.result, own_h), local.at[self.k]
                )
                self.copy.start()
            else:
                self.s3 = tuple(
                    start(self.at(b, z, lo, H), stage.at[self.k, i], peer)
                    for i, (lo, peer) in enumerate(((0, XP), (H, XM)))
                )

        def relay(self):
            arrived(self.s3[0], stage.at[self.k, 0])
            s0 = start(stage.at[self.k, 0], self.half(self.result, mh, 0, H), XP, "x", self.k)
            arrived(self.s3[1], stage.at[self.k, 1])
            s1 = start(stage.at[self.k, 1], self.half(self.result, ph, H, H), XM, "x", self.k)
            self.s4 = s0, s1

        def whole(self):
            self.copy.wait()
            arrived(self.s4[0], self.half(self.result, other_h))

    def transpose_tokens():
        @pl.loop(0, D // 256)
        def _(j):
            at = pl.ds(mult(j * 256, 256), 256)
            tok_t[at, :] = tok[:, at].T

    def hidden(j):
        at = pl.ds(j * 256, 256)
        for lo in range(0, TOK, 256):
            rows = pl.ds(lo, 256)
            pre = dot(tok[rows, :], w1[:, at])
            cdf = 0.5 * (1.0 + lax.erf(pre * inv_root_two))
            value = (pre * cdf).astype(BF16)
            act[rows, at] = value
            act_t[at, rows] = value.T
            slope[rows, at] = cdf + pre * jnp.exp(-0.5 * pre * pre) * inv_root_tau

    def output_terms(yv):
        oterm[:, line(yv)] = dot(act[...], w2[:, line(yv)]).astype(BF16)

    def second_terms(zv, b):
        at = pl.ds(mult(((own_h, other_h)[b] * 4 + zv) * B, 128), B)
        p2[:, at] = dot(act_t[...], cot[:, at]).astype(BF16)

    def hidden_grad(j):
        at = pl.ds(j * 256, 256)
        for lo in range(0, TOK, 256):
            rows = pl.ds(lo, 256)
            back = dot_nt(cot[rows, :], w2[at, :])
            hg[rows, at] = (back * slope[rows, at]).astype(BF16)

    def first_terms(zv, b):
        at = pl.ds(mult(((own_h, other_h)[b] * 4 + zv) * B, 128), B)
        p1[at, :] = dot(tok_t[at, :], hg[...]).astype(BF16)

    def input_terms(yv):
        tok[:, line(yv)] = dot_nt(hg[...], w1[line(yv), :]).astype(BF16)

    of_theirs = pl.ds(mult(oc * B, 128), B)
    wf = Weights(0, w1_in, w1, loc1, half1, w1.at[:, of_theirs])
    ws = Weights(1, w2_in, w2, loc2, half2, w2.at[of_theirs, :])
    gt = Gather(tok_in, tok, 0)
    gc = Gather(cot_in, cot, 1)
    po = Plane(oterm, 0, out_ref)
    pi = Plane(tok, 1, ing_ref)
    gs = Grad(2, p2, loc2, rsw2, rza2, rzb2, g2_ref, half2)
    gf = Grad(3, p1, loc1, rsw1, rza1, rzb1, g1_ref, half1)
    gt.swap()
    wf.own()
    gc.swap()
    wf.exchange()
    gt.assemble()
    ws.own()
    gt.b.own_first()
    gt.a.own_first()
    gc.assemble()
    gc.b.own_first()
    gc.a.both("o")
    gt.a.both("o")
    wf.relay()
    wf.forward(OWN)
    ws.exchange()
    gt.a.near("p")
    gt.a.near("m")
    wf.partner()
    ws.relay()
    gc.a.own_first()
    gt.b.near("p")
    gc.b.near("p")
    gc.b.near("m")
    gt.a.forward("p")
    gt.b.near("m")
    gt.a.far()
    gt.a.forward("o")
    ws.partner()
    ws.forward(OWN)
    wf.last(OWN)
    gc.a.near("m")
    gt.b.both("o")
    gt.a.forward("t")
    gt.b.far()
    gc.a.near("p")
    wf.forward(OTHER)
    gt.a.forward("m")
    gt.b.forward("p")
    gt.b.forward("m")
    gc.a.far()
    gc.b.far()
    gt.b.forward("o")
    gt.b.forward("t")
    ws.forward(OTHER)
    gc.a.forward("o")
    gc.b.forward("m")
    gc.b.both("o")
    gc.b.forward("t")
    wf.last(OTHER)
    gt.whole()
    gc.a.forward("p")
    transpose_tokens()
    gc.b.forward("p")
    wf.whole()
    hidden(2)
    gc.a.forward("m")
    gc.a.forward("t")
    gc.b.forward("o")
    hidden(1)
    ws.last(OWN)
    ws.last(OTHER)
    hidden(0)
    gt.flush()
    ws.whole()
    output_terms(y2)
    gc.whole()
    po.a.far("o")
    second_terms(z2, OTHER)
    gs.swap(0, z2, OTHER)
    po.a.far("t")
    second_terms(zp, OTHER)
    gs.swap(1, zp, OTHER)
    output_terms(yp)
    po.a.far("m")
    output_terms(ym)
    gs.swapped(0, z2, OTHER)
    gs.far(OTHER)
    gs.early(OTHER)
    po.b.far("p")
    po.b.far("t")
    po.b.far("m")
    po.a.early("t")
    po.b.early("m")
    po.a.early("p")
    po.a.far("p")
    hidden_grad(0)
    po.b.early("p")
    hidden_grad(2)
    po.b.early("t")
    po.a.near("t")
    hidden_grad(1)
    po.a.early("m")
    po.b.near("m")
    first_terms(z2, OTHER)
    gf.swap(0, z2, OTHER)
    first_terms(zp, OTHER)
    po.b.near("p")
    gf.swap(1, zp, OTHER)
    input_terms(y2)
    pi.b.early("t")
    po.b.near("t")
    input_terms(ym)
    pi.b.far("m")
    gf.swapped(0, z2, OTHER)
    gf.far(OTHER)
    pi.b.far("t")
    gf.early(OTHER)
    output_terms(y)
    po.b.far("o")
    second_terms(zm, OTHER)
    po.a.near("p")
    po.a.near("m")
    gs.swap(2, zm, OTHER)
    po.a.first_far()
    second_terms(z2, OWN)
    gs.swap(0, z2, OWN)
    pi.a.far("t")
    second_terms(z, OTHER)
    po.b.early("o")
    input_terms(yp)
    pi.b.early("p")
    first_terms(zm, OTHER)
    pi.b.far("p")
    gs.swapped(0, z2, OWN)
    pi.b.near("t")
    po.b.first_far()
    gs.far(OWN)
    first_terms(z2, OWN)
    pi.a.far("m")
    po.b.near("o")
    gf.swap(2, zm, OTHER)
    gs.near(OTHER)
    gs.swap(3, z, OTHER)
    pi.a.far("o")
    second_terms(zm, OWN)
    pi.b.early("m")
    first_terms(zp, OWN)
    input_terms(y)
    gf.swap(1, zp, OWN)
    pi.b.early("o")
    gs.swap(2, zm, OWN)
    pi.b.far("o")
    second_terms(zp, OWN)
    po.a.first_near("p")
    first_terms(zm, OWN)
    po.a.first_near("m")
    gf.near(OTHER)
    gf.swap(0, z2, OWN)
    pi.a.far("p")
    po.b.first_near("p")
    pi.a.early("t")
    pi.b.first_far()
    gs.swap(1, zp, OWN)
    gf.swap(2, zm, OWN)
    first_terms(z, OTHER)
    pi.b.near("o")
    gf.swapped(0, z2, OWN)
    gf.far(OWN)
    pi.a.near("t")
    first_terms(z, OWN)
    gf.swap(3, z, OWN)
    pi.b.near("p")
    pi.a.early("m")
    pi.a.early("p")
    gf.swap(3, z, OTHER)
    gs.early(OWN)
    second_terms(z, OWN)
    pi.b.near("m")
    gs.swap(3, z, OWN)
    gs.total(OTHER)
    gs.near(OWN)
    pi.a.first_far()
    pi.a.near("m")
    pi.b.first_near("p")
    pi.a.near("p")
    gs.relay()
    gf.early(OWN)
    gf.total(OTHER)
    po.b.first_near("m")
    pi.a.early("o")
    pi.b.first_near("m")
    gf.near(OWN)
    pi.a.first_near("m")
    pi.a.near("o")
    po.a.early("o")
    po.a.near("o")
    pi.a.first_near("p")
    gf.relay()
    pi.done()
    gs.total(OWN)
    po.done()
    gf.total(OWN)
    for part in (po, gs, gf, pi):
        part.whole()
    links.flush(0)


def widen(out_in, ing_in, g1_in, g2_in, out_ref, ing_ref, g1_ref, g2_ref):
    out_ref[...] = out_in[...]
    ing_ref[...] = ing_in[...]
    g1_ref[...] = g1_in[...].astype(F32)
    g2_ref[...] = g2_in[...].astype(F32)


def shards(tokens, w_first, w_second, cotangent):
    hbm = pl.BlockSpec(memory_space=pl.ANY)
    parts = pl.pallas_call(
        kernel,
        name="mlp",
        out_shape=(
            jax.ShapeDtypeStruct((192, TOK), BF16),
            jax.ShapeDtypeStruct((192, TOK), BF16),
            jax.ShapeDtypeStruct((B, 2 * B), BF16),
            jax.ShapeDtypeStruct((2 * B, B), BF16),
        ),
        in_specs=[hbm] * 4,
        out_specs=(hbm,) * 4,
        scratch_shapes=[
            pltpu.VMEM((D, HID), BF16),
            pltpu.VMEM((HID, D), BF16),
            pltpu.VMEM((TOK, D), BF16),
            pltpu.VMEM((TOK, D), BF16),
            pltpu.VMEM((D, TOK), BF16),
            pltpu.VMEM((TOK, HID), BF16),
            pltpu.VMEM((HID, TOK), BF16),
            pltpu.VMEM((TOK, HID), F32),
            pltpu.VMEM((TOK, HID), BF16),
            pltpu.VMEM((TOK, D), BF16),
            pltpu.VMEM((D, HID), BF16),
            pltpu.VMEM((HID, D), BF16),
            pltpu.VMEM((4, 2, B, B), BF16),
            pltpu.VMEM((4, 2, B, B), BF16),
            pltpu.VMEM((2, B, B), BF16),
            pltpu.VMEM((2, B, B), BF16),
            pltpu.VMEM((2, 2, B, B), BF16),
            pltpu.VMEM((2, 2, B, B), BF16),
            pltpu.VMEM((2, 4, RA, B), BF16),
            pltpu.VMEM((2, 2, 4, RA, B), BF16),
            pltpu.VMEM((2, 2, SPLIT_A[0], B), BF16),
            pltpu.VMEM((2, 2, RA, B), BF16),
            pltpu.VMEM((2, 4, RB, B), BF16),
            pltpu.VMEM((2, 2, 4, RB, B), BF16),
            pltpu.VMEM((2, 2, SPLIT_B[0], B), BF16),
            pltpu.VMEM((2, 2, RB, B), BF16),
            pltpu.VMEM((2, 192, HALF), BF16),
            pltpu.VMEM((2, 192, HALF), BF16),
            pltpu.VMEM((4, 2, B // 2, B), BF16),
            pltpu.VMEM((2, 192, TOK), BF16),
            pltpu.VMEM((2, 192, HALF), BF16),
            pltpu.SemaphoreType.DMA((2,)),
            pltpu.SemaphoreType.DMA((NSEM,)),
            pltpu.SemaphoreType.DMA((8,)),
        ],
        compiler_params=pltpu.CompilerParams(
            collective_id=0, has_side_effects=True, vmem_limit_bytes=60 * 1024 * 1024
        ),
        cost_estimate=pl.CostEstimate(flops=14_500_000_000, bytes_accessed=40_000_000, transcendentals=800_000),
    )(tokens.T, cotangent.T, w_first, w_second)
    steps = 2
    specs = [pl.BlockSpec((part.shape[0] // steps, part.shape[1]), lambda i: (i, 0)) for part in parts]
    outputs, input_grad, first_grad, second_grad = pl.pallas_call(
        widen,
        name="widen",
        grid=(steps,),
        out_shape=[
            jax.ShapeDtypeStruct(part.shape, dtype) for part, dtype in zip(parts, (BF16, BF16, F32, F32))
        ],
        in_specs=specs,
        out_specs=specs,
    )(*parts)
    return outputs.T, input_grad.T, first_grad, second_grad


def solution(mesh):
    finer = Mesh(mesh.devices.reshape(2, 4, 4, 2, 2), AXES)
    in_specs = (P(DP, MP), P(DP, MP), P(MP, DP), P(DP, MP))
    out_specs = (P(DP, MP), P(DP, MP), P(DP, MP), P(MP, DP))
    return jax.shard_map(
        shards, mesh=finer, in_specs=in_specs, out_specs=out_specs, check_vma=False
    )
```

```python
import jax
import jax.numpy as jnp
from jax import lax
from jax.experimental import pallas as pl
from jax.experimental.pallas import tpu as pltpu
from jax.sharding import Mesh
from jax.sharding import PartitionSpec as P

AXES = ("xh", "z", "y", "xl", "c")
DP = ("xh", "z")
MP = ("y", "xl", "c")
MESH = pl.DeviceIdType.MESH
F32 = jnp.float32
BF16 = jnp.bfloat16

D = 3072
B = 384
HID = 768
TOK = 512
HALF = 256
RA = 176
RB = HALF - RA
SPLIT_A = (96, 80)
SPLIT_B = (48, 32)
NSEM = 156

inv_root_two = 0.7071067811865476
inv_root_tau = 0.3989422804014327


def dot(a, b):
    return jnp.dot(a, b, preferred_element_type=F32)


def dot_nt(a, b):
    return lax.dot_general(a, b, (((1,), (1,)), ((), ())), preferred_element_type=F32)


def dot_tn(a, b):
    return lax.dot_general(a, b, (((0,), (0,)), ((), ())), preferred_element_type=F32)


def mult(value, of):
    return pl.multiple_of(value, of)


class Links:
    def __init__(self, send, recv, early):
        self.send, self.recv, self.early, self.count = send, recv, early, 0
        self.open, self.flushed = ([], []), False
        self.sems, self.shared = 0, {}

    def start(self, src, dst, peer, *share):
        i = self.count
        self.count += 1
        sem = self.shared.get(share, self.sems)
        if sem == self.sems:
            self.sems += 1
        if share:
            self.shared[share] = sem
        group = int(getattr(src, "ref", src) is self.early and not self.flushed)
        copy = pltpu.make_async_remote_copy(
            src_ref=src,
            dst_ref=dst,
            send_sem=self.send.at[group],
            recv_sem=self.recv.at[sem],
            device_id=peer,
            device_id_type=MESH,
        )
        copy.start()
        self.open[group].append(copy)
        return i, peer, sem

    def arrived(self, handle, where):
        i, peer, sem = handle
        pltpu.make_async_remote_copy(
            src_ref=where,
            dst_ref=where,
            send_sem=self.send.at[0],
            recv_sem=self.recv.at[sem],
            device_id=peer,
            device_id_type=MESH,
        ).wait_recv()

    def flush(self, group):
        for copy in self.open[group]:
            copy.wait_send()
        self.flushed = True


def kernel(
    tok_in, cot_in, w1_in, w2_in,
    out_ref, ing_ref, g1_ref, g2_ref,
    w1, w2, tok, cot, tok_t, act, act_t, slope, hg, oterm, p1, p2,
    rsw1, rsw2, rza1, rza2, rzb1, rzb2,
    ra1, ra2, ra3, ra4, rb1, rb2, rb3, rb4,
    swap_in, swap_out, stage, shards, results, send, recv, local,
):
    xh, z, y, xl, c = (lax.axis_index(a) for a in AXES)
    x = xh * 2 + xl
    xp, xm = lax.rem(x + 1, 4), lax.rem(x + 3, 4)
    ph, pll = xp // 2, lax.rem(xp, 2)
    mh, ml = xm // 2, lax.rem(xm, 2)
    yp, ym, y2 = lax.rem(y + 1, 4), lax.rem(y + 3, 4), lax.rem(y + 2, 4)
    zp, zm, z2 = lax.rem(z + 1, 4), lax.rem(z + 3, 4), lax.rem(z + 2, 4)
    oc = 1 - c
    XP, XM = {"xh": ph, "xl": pll}, {"xh": mh, "xl": ml}
    YP, YM, ZP, ZM, OC = {"y": yp}, {"y": ym}, {"z": zp}, {"z": zm}, {"c": oc}
    H = B // 2
    OWN, OTHER = 0, 1
    own_h, other_h = xh, 1 - xh
    links = Links(send, recv, tok)
    start, arrived = links.start, links.arrived

    loads = [
        pltpu.make_async_copy(ref, shards.at[k], local.at[4 + k]) for k, ref in enumerate((tok_in, cot_in))
    ]
    for load in loads:
        load.start()
    bar = pltpu.get_barrier_semaphore()
    for peer in (XP, XM, YP, YM, ZP, ZM, OC):
        pl.semaphore_signal(bar, inc=1, device_id=peer, device_id_type=MESH)
    pl.semaphore_wait(bar, 7)

    def rows_a(hv, lo=0, n=RA):
        return pl.ds(mult(hv * RA + lo, 16), n)

    def rows_b(hv, lo=0, n=RB):
        return pl.ds(mult(2 * RA + hv * RB + lo, 16), n)

    def cols(yv, lv):
        return pl.ds(mult((yv * 2 + lv) * B, 128), B)

    def line(yv):
        return pl.ds(mult(yv * 2 * B, 128), 2 * B)

    def loc1(ref, hv, zv, cv, lo=0, n=B):
        return ref.at[pl.ds(mult((hv * 4 + zv) * B + lo, 64), n), pl.ds(mult(cv * B, 128), B)]

    def loc2(ref, hv, zv, cv, lo=0, n=B):
        return ref.at[pl.ds(mult(cv * B + lo, 64), n), pl.ds(mult((hv * 4 + zv) * B, 128), B)]

    def half1(ref, hv, lo=0, n=B):
        return ref.at[pl.ds(lo, n), pl.ds(mult(hv * B, 128), B)]

    def half2(ref, hv, lo=0, n=B):
        return ref.at[pl.ds(mult(hv * B + lo, 64), n), :]

    class Weights:
        def __init__(self, k, shard, ref, loc, half, theirs):
            self.at = lambda b, zv, *part: loc(ref, (own_h, other_h)[b], zv, c, *part)
            self.theirs = theirs
            self.relayed = lambda hv, *part: loc(ref, hv, z, c, *part)
            self.swaps, self.z1, self.z2 = [], {}, {}
            self.k, self.shard, self.half = k, shard, half

        def swap(self, b, zv, src=None):
            block = self.at(b, zv)
            self.swaps.append(start(block if src is None else src, block, OC, "w", self.k))

        def exchange(self):
            self.x1 = tuple(
                start(self.half(self.shard, other_h, lo, H), stage.at[self.k, i], peer)
                for i, (lo, peer) in enumerate(((0, XP), (H, XM)))
            )

        def relay(self):
            arrived(self.x1[0], stage.at[self.k, 0])
            s0 = start(stage.at[self.k, 0], self.relayed(mh, 0, H), XP, "x", self.k)
            arrived(self.x1[1], stage.at[self.k, 1])
            s1 = start(stage.at[self.k, 1], self.relayed(ph, H, H), XM, "x", self.k)
            self.x2 = s0, s1

        def own(self):
            src, dst = self.half(self.shard, own_h), self.at(OWN, z)
            self.z1[OWN] = start(src, dst, ZP), start(src, dst, ZM)
            self.swap(OWN, z, src)
            self.copy = pltpu.make_async_copy(src, dst, local.at[self.k])
            self.copy.start()

        def partner(self):
            block = self.at(OTHER, z)
            arrived(self.x2[0], block)
            self.z1[OTHER] = start(block, block, ZP), start(block, block, ZM)
            self.swap(OTHER, z)

        def forward(self, b):
            p, m = self.z1[b]
            from_m, from_p = self.at(b, zm), self.at(b, zp)
            if b == OWN:
                arrived(p, from_m)
                self.z2[b] = start(from_m, from_m, ZP)
                arrived(m, from_p)
            else:
                arrived(m, from_p)
                self.z2[b] = start(from_p, from_p, ZM)
                arrived(p, from_m)
            self.swap(b, zm)
            self.swap(b, zp)

        def last(self, b):
            arrived(self.z2[b], self.at(b, z2))
            self.swap(b, z2)

        def whole(self):
            self.copy.wait()
            arrived(self.swaps[0], self.theirs)

    xs = {"o": (xh, xl), "m": (mh, ml), "p": (ph, pll), "t": (1 - xh, xl)}
    ys = {"o": y, "m": ym, "p": yp, "t": y2}
    PLUS = "om"

    def place_a(ref, i, j, lo=0, n=RA):
        (hv, lv), yv = xs[i], ys[j]
        return ref.at[rows_a(hv, lo, n), cols(yv, lv)]

    def place_b(ref, i, j, lo=0, n=RB):
        (hv, lv), yv = xs[j], ys[i]
        return ref.at[rows_b(hv, lo, n), cols(yv, lv)]

    ROUTES = {"a": (place_a, SPLIT_A, (XP, XM), (YP, YM)), "b": (place_b, SPLIT_B, (YP, YM), (XP, XM))}

    pick_row = lax.broadcasted_iota(jnp.int32, (192, B), 0)
    pick_col = lax.broadcasted_iota(jnp.int32, (192, B), 1)
    ours = (pick_col == pick_row + 192 * c).astype(BF16)
    theirs = (pick_col == pick_row + 192 * oc).astype(BF16)

    class GatherPart:
        def __init__(self, ref, route, k):
            self.route, self.k, self.key = route, k, ("g", k) if route == "a" else ()
            self.far_line = ref.at[pl.ds(0, 2 * RA), line(y2)]
            place, self.split, self.first, self.second = ROUTES[route]
            self.at = lambda *where: place(ref, *where)
            self.f2, self.s1, self.s2 = {}, {}, {}

        def both(self, i):
            block = self.at(i, "o")
            self.s1[i] = tuple(start(block, block, peer) for peer in self.second)

        def own_first(self):
            block = self.at("o", "o")
            self.f1 = tuple(start(block, block, peer) for peer in self.first)

        def near(self, i):
            n0, n1 = self.split
            p, m = self.first
            if i == "m":
                arrived(self.f1[0], self.at("m", "o"))
                block = self.at("m", "o", 0, n0)
                self.f2[0] = start(block, block, p, "f", self.route, self.k)
            else:
                arrived(self.f1[1], self.at("p", "o"))
                block = self.at("p", "o", n0, n1)
                self.f2[1] = start(block, block, m, "f", self.route, self.k)
            self.both(i)

        def far(self):
            arrived(self.f2[0], self.at("t", "o"))
            self.both("t")

        def forward(self, i):
            from_m, from_p = self.at(i, "m"), self.at(i, "p")
            if i in PLUS:
                arrived(self.s1[i][0], from_m)
                self.s2[i] = start(from_m, from_m, self.second[0], *self.key)
                arrived(self.s1[i][1], from_p)
            else:
                arrived(self.s1[i][1], from_p)
                self.s2[i] = start(from_p, from_p, self.second[1], *self.key)
                arrived(self.s1[i][0], from_m)

        def whole(self):
            if self.key:
                arrived(self.s2["o"], self.far_line)
            else:
                for i in "ompt":
                    arrived(self.s2[i], self.at(i, "t"))

    class Gather:
        def __init__(self, shard, ref, k):
            self.ref, self.shard, self.k = ref, shard, k
            self.a, self.b = GatherPart(ref, "a", k), GatherPart(ref, "b", k)

        def swap(self):
            src = self.shard.at[:, pl.ds(mult(oc * HALF, HALF), HALF)]
            self.swapped = start(src, swap_in.at[self.k], OC)

        def assemble(self):
            arrived(self.swapped, swap_in.at[self.k])
            loads[self.k].wait()
            mine = shards[self.k, :, pl.ds(mult(c * HALF, HALF), HALF)]
            block = (dot_tn(mine, ours) + dot_tn(swap_in[self.k], theirs)).astype(BF16)
            self.ref[rows_a(xh), cols(y, xl)] = block[:RA]
            self.ref[rows_b(xh), cols(y, xl)] = block[RA:]

        def whole(self):
            self.a.whole()
            self.b.whole()

        def flush(self):
            links.flush(1)

    def add_into(where, *parts):
        total = where[...].astype(F32)
        for part in parts:
            total = total + part.astype(F32)
        where[...] = total.astype(BF16)

    class SumPart:
        def __init__(self, ref, route, k, r1, r2, r3, r4):
            place, self.split, self.first, self.second = ROUTES[route]
            self.at = lambda *where: place(ref, *where)
            self.key = "s", route, k
            self.r1, self.r2, self.r3, self.r4 = r1.at[k], r2.at[k], r3.at[k], r4.at[k]
            self.s0, self.s1, self.s2, self.s4 = {}, {}, {}, {}

        def far(self, i):
            n = "ompt".index(i)
            peer = self.second[0] if i in PLUS else self.second[1]
            self.s1[i] = start(self.at(i, "t"), self.r1.at[n], peer)

        def early(self, i):
            n = "ompt".index(i)
            if i in PLUS:
                self.s0[i] = start(self.at(i, "m"), self.r2.at[1, n], self.second[1], *self.key, i)
            else:
                self.s0[i] = start(self.at(i, "p"), self.r2.at[0, n], self.second[0], *self.key, i)

        def near(self, i):
            n = "ompt".index(i)
            arrived(self.s1[i], self.r1.at[n])
            if i in PLUS:
                add_into(self.at(i, "p"), self.r1[n])
                p = start(self.at(i, "p"), self.r2.at[0, n], self.second[0], *self.key, i)
                self.s2[i] = p, self.s0[i]
            else:
                add_into(self.at(i, "m"), self.r1[n])
                m = start(self.at(i, "m"), self.r2.at[1, n], self.second[1], *self.key, i)
                self.s2[i] = self.s0[i], m

        def summed(self, i, wait=True):
            n = "ompt".index(i)
            if wait:
                arrived(self.s2[i][0], self.r2.at[:, n])
            return self.r2[0, n], self.r2[1, n]

        def first_far(self):
            add_into(self.at("t", "o"), *self.summed("t"))
            n0, n1 = self.split
            self.s3 = (
                start(self.at("t", "o", 0, n0), self.r3.at[0, pl.ds(0, n0)], self.first[0]),
                start(self.at("t", "o", n0, n1), self.r3.at[1, pl.ds(0, n1)], self.first[1]),
            )

        def first_near(self, i):
            n0, n1 = self.split
            if i == "p":
                arrived(self.s3[0], self.r3.at[0, pl.ds(0, n0)])
                add_into(self.at("p", "o", n0, n1), *(r[n0:] for r in self.summed("p")))
                add_into(self.at("p", "o", 0, n0), self.r3[0, :n0], *(r[:n0] for r in self.summed("p", False)))
                self.s4[0] = start(self.at("p", "o"), self.r4.at[0], self.first[0])
            else:
                arrived(self.s3[1], self.r3.at[1, pl.ds(0, n1)])
                add_into(self.at("m", "o", 0, n0), *(r[:n0] for r in self.summed("m")))
                add_into(self.at("m", "o", n0, n1), self.r3[1, :n1], *(r[n0:] for r in self.summed("m", False)))
                self.s4[1] = start(self.at("m", "o"), self.r4.at[1], self.first[1])

        def total(self):
            parts = self.summed("o")
            arrived(self.s4[0], self.r4.at[0])
            arrived(self.s4[1], self.r4.at[1])
            value = self.at("o", "o")[...].astype(F32)
            for part in (*parts, self.r4[0], self.r4[1]):
                value = value + part.astype(F32)
            return value.astype(BF16)

    class Plane:
        def __init__(self, ref, k, result):
            self.k, self.result = k, result
            self.a = SumPart(ref, "a", k, ra1, ra2, ra3, ra4)
            self.b = SumPart(ref, "b", k, rb1, rb2, rb3, rb4)

        def done(self):
            k = self.k
            total = jnp.concatenate([self.a.total(), self.b.total()], axis=0)
            mine = pl.ds(mult(c * HALF, HALF), HALF)
            swap_out[k] = dot_nt(theirs, total).astype(BF16)
            self.last = start(swap_out.at[k], self.result.at[:, mine], OC)
            results[k] = dot_nt(ours, total).astype(BF16)
            self.copy = pltpu.make_async_copy(results.at[k], self.result.at[:, mine], local.at[6 + k])
            self.copy.start()

        def whole(self):
            self.copy.wait()
            arrived(self.last, self.result.at[:, pl.ds(mult(oc * HALF, HALF), HALF)])

    class Grad:
        def __init__(self, k, ref, loc, rsw, rz1, rz2, result, half):
            self.at = lambda b, zv, *part: loc(ref, (own_h, other_h)[b], zv, c, *part)
            self.theirs = lambda b, zv: loc(ref, (own_h, other_h)[b], zv, oc)
            self.k, self.rsw, self.rz1, self.rz2, self.result, self.half = k, rsw, rz1, rz2, result, half
            self.swaps, self.s0, self.s1, self.s2 = {}, {}, {}, {}

        def swap(self, j, zv, b):
            self.swaps[j, b] = start(self.theirs(b, zv), self.rsw.at[j, b], OC)

        def swapped(self, j, zv, b):
            arrived(self.swaps[j, b], self.rsw.at[j, b])
            add_into(self.at(b, zv), self.rsw[j, b])

        def far(self, b):
            self.s1[b] = start(self.at(b, z2), self.rz1.at[b], ZP if b == OWN else ZM)

        def early(self, b):
            if b == OWN:
                self.swapped(2, zm, b)
                self.s0[b] = start(self.at(b, zm), self.rz2.at[1, b], ZM, "t", self.k, b)
            else:
                self.swapped(1, zp, b)
                self.s0[b] = start(self.at(b, zp), self.rz2.at[0, b], ZP, "t", self.k, b)

        def near(self, b):
            arrived(self.s1[b], self.rz1.at[b])
            j, zv = (1, zp) if b == OWN else (2, zm)
            arrived(self.swaps[j, b], self.rsw.at[j, b])
            add_into(self.at(b, zv), self.rsw[j, b], self.rz1[b])
            if b == OWN:
                self.s2[b] = start(self.at(b, zp), self.rz2.at[0, b], ZP, "t", self.k, b), self.s0[b]
            else:
                self.s2[b] = self.s0[b], start(self.at(b, zm), self.rz2.at[1, b], ZM, "t", self.k, b)

        def total(self, b):
            arrived(self.s2[b][0], self.rz2.at[:, b])
            arrived(self.swaps[3, b], self.rsw.at[3, b])
            add_into(self.at(b, z), self.rsw[3, b], self.rz2[0, b], self.rz2[1, b])
            if b == OWN:
                self.copy = pltpu.make_async_copy(
                    self.at(b, z), self.half(self.result, own_h), local.at[self.k]
                )
                self.copy.start()
            else:
                self.s3 = tuple(
                    start(self.at(b, z, lo, H), stage.at[self.k, i], peer)
                    for i, (lo, peer) in enumerate(((0, XP), (H, XM)))
                )

        def relay(self):
            arrived(self.s3[0], stage.at[self.k, 0])
            s0 = start(stage.at[self.k, 0], self.half(self.result, mh, 0, H), XP, "x", self.k)
            arrived(self.s3[1], stage.at[self.k, 1])
            s1 = start(stage.at[self.k, 1], self.half(self.result, ph, H, H), XM, "x", self.k)
            self.s4 = s0, s1

        def whole(self):
            self.copy.wait()
            arrived(self.s4[0], self.half(self.result, other_h))

    def transpose_tokens():
        @pl.loop(0, D // 256)
        def _(j):
            at = pl.ds(mult(j * 256, 256), 256)
            tok_t[at, :] = tok[:, at].T

    def hidden(j):
        at = pl.ds(j * 256, 256)
        for lo in range(0, TOK, 256):
            rows = pl.ds(lo, 256)
            pre = dot(tok[rows, :], w1[:, at])
            cdf = 0.5 * (1.0 + lax.erf(pre * inv_root_two))
            value = (pre * cdf).astype(BF16)
            act[rows, at] = value
            act_t[at, rows] = value.T
            slope[rows, at] = cdf + pre * jnp.exp(-0.5 * pre * pre) * inv_root_tau

    def output_terms(yv):
        oterm[:, line(yv)] = dot(act[...], w2[:, line(yv)]).astype(BF16)

    def second_terms(zv, b):
        at = pl.ds(mult(((own_h, other_h)[b] * 4 + zv) * B, 128), B)
        p2[:, at] = dot(act_t[...], cot[:, at]).astype(BF16)

    def hidden_grad(j):
        at = pl.ds(j * 256, 256)
        for lo in range(0, TOK, 256):
            rows = pl.ds(lo, 256)
            back = dot_nt(cot[rows, :], w2[at, :])
            hg[rows, at] = (back * slope[rows, at]).astype(BF16)

    def first_terms(zv, b):
        at = pl.ds(mult(((own_h, other_h)[b] * 4 + zv) * B, 128), B)
        p1[at, :] = dot(tok_t[at, :], hg[...]).astype(BF16)

    def input_terms(yv):
        tok[:, line(yv)] = dot_nt(hg[...], w1[line(yv), :]).astype(BF16)

    of_theirs = pl.ds(mult(oc * B, 128), B)
    wf = Weights(0, w1_in, w1, loc1, half1, w1.at[:, of_theirs])
    ws = Weights(1, w2_in, w2, loc2, half2, w2.at[of_theirs, :])
    gt = Gather(tok_in, tok, 0)
    gc = Gather(cot_in, cot, 1)
    po = Plane(oterm, 0, out_ref)
    pi = Plane(tok, 1, ing_ref)
    gs = Grad(2, p2, loc2, rsw2, rza2, rzb2, g2_ref, half2)
    gf = Grad(3, p1, loc1, rsw1, rza1, rzb1, g1_ref, half1)
    wf.exchange()
    gt.swap()
    gc.swap()
    wf.own()
    ws.own()
    gt.assemble()
    gt.b.own_first()
    gt.a.own_first()
    gc.assemble()
    gt.a.both("o")
    wf.relay()
    ws.exchange()
    gc.b.own_first()
    gc.a.both("o")
    gt.a.near("m")
    gt.a.near("p")
    wf.partner()
    wf.forward(OWN)
    ws.relay()
    gc.a.own_first()
    gt.a.forward("m")
    gt.b.near("m")
    gc.b.near("p")
    gt.a.far()
    gt.b.near("p")
    ws.partner()
    gt.a.forward("p")
    wf.forward(OTHER)
    gt.b.far()
    ws.forward(OWN)
    gt.b.both("o")
    gc.a.near("m")
    gc.a.near("p")
    gt.b.forward("m")
    gc.b.near("m")
    gt.a.forward("o")
    gt.a.forward("t")
    gt.b.forward("t")
    gt.b.forward("p")
    gt.b.forward("o")
    gc.a.far()
    wf.last(OWN)
    ws.forward(OTHER)
    gc.a.forward("m")
    gc.b.far()
    gc.b.both("o")
    wf.last(OTHER)
    gt.whole()
    gc.a.forward("p")
    gc.b.forward("m")
    gc.a.forward("o")
    transpose_tokens()
    gc.b.forward("t")
    wf.whole()
    hidden(0)
    gc.b.forward("p")
    gc.b.forward("o")
    gc.a.forward("t")
    hidden(2)
    ws.last(OWN)
    ws.last(OTHER)
    hidden(1)
    ws.whole()
    output_terms(y2)
    gt.flush()
    po.a.far("t")
    gc.whole()
    po.b.far("t")
    po.b.early("t")
    po.a.far("m")
    second_terms(z2, OTHER)
    gs.swap(0, z2, OTHER)
    second_terms(zp, OTHER)
    gs.swap(1, zp, OTHER)
    output_terms(ym)
    output_terms(yp)
    gs.swapped(0, z2, OTHER)
    gs.far(OTHER)
    po.a.early("m")
    po.a.early("t")
    po.b.early("m")
    po.b.far("m")
    po.a.far("p")
    po.b.early("p")
    po.a.early("p")
    po.b.far("p")
    po.a.far("o")
    po.b.near("t")
    gs.early(OTHER)
    hidden_grad(0)
    hidden_grad(1)
    hidden_grad(2)
    first_terms(z2, OTHER)
    gf.swap(0, z2, OTHER)
    po.b.near("m")
    first_terms(zp, OTHER)
    gf.swap(1, zp, OTHER)
    po.a.near("t")
    input_terms(y2)
    pi.b.far("t")
    pi.b.early("t")
    input_terms(yp)
    gf.swapped(0, z2, OTHER)
    pi.b.far("p")
    gf.far(OTHER)
    po.b.near("p")
    pi.a.far("t")
    pi.b.early("p")
    pi.a.early("t")
    second_terms(z2, OWN)
    gf.early(OTHER)
    output_terms(y)
    gs.swap(0, z2, OWN)
    po.b.far("o")
    input_terms(y)
    pi.b.far("o")
    po.b.first_far()
    second_terms(zm, OTHER)
    pi.b.near("t")
    second_terms(z, OWN)
    gs.swapped(0, z2, OWN)
    gs.swap(2, zm, OTHER)
    first_terms(zm, OTHER)
    po.a.first_far()
    first_terms(zm, OWN)
    po.a.near("m")
    po.a.near("p")
    pi.b.early("o")
    gf.swap(2, zm, OTHER)
    gs.swap(3, z, OWN)
    pi.b.near("p")
    gs.far(OWN)
    input_terms(ym)
    po.b.early("o")
    pi.b.far("m")
    gs.near(OTHER)
    pi.b.early("m")
    first_terms(z, OWN)
    gf.swap(2, zm, OWN)
    pi.b.near("o")
    first_terms(z2, OWN)
    gf.swap(3, z, OWN)
    pi.b.first_far()
    second_terms(zm, OWN)
    pi.a.far("m")
    po.b.near("o")
    gs.swap(2, zm, OWN)
    first_terms(z, OTHER)
    pi.a.far("o")
    gf.swap(0, z2, OWN)
    pi.a.near("t")
    pi.a.far("p")
    pi.a.early("m")
    first_terms(zp, OWN)
    pi.b.near("m")
    po.b.first_near("m")
    second_terms(zp, OWN)
    gf.near(OTHER)
    gf.swap(3, z, OTHER)
    second_terms(z, OTHER)
    po.b.first_near("p")
    pi.a.early("p")
    gf.swapped(0, z2, OWN)
    gf.swap(1, zp, OWN)
    gf.far(OWN)
    po.a.first_near("m")
    po.a.first_near("p")
    gs.early(OWN)
    gs.swap(3, z, OTHER)
    gs.swap(1, zp, OWN)
    pi.b.first_near("m")
    gf.early(OWN)
    gs.total(OTHER)
    pi.a.first_far()
    pi.a.near("p")
    pi.a.near("m")
    gs.relay()
    gs.near(OWN)
    gf.total(OTHER)
    pi.a.early("o")
    gf.near(OWN)
    pi.a.near("o")
    pi.a.first_near("p")
    pi.a.first_near("m")
    pi.b.first_near("p")
    po.a.early("o")
    po.a.near("o")
    gs.total(OWN)
    gf.relay()
    pi.done()
    po.done()
    gf.total(OWN)
    for part in (po, gs, gf, pi):
        part.whole()
    links.flush(0)


def widen(out_in, ing_in, g1_in, g2_in, out_ref, ing_ref, g1_ref, g2_ref):
    out_ref[...] = out_in[...]
    ing_ref[...] = ing_in[...]
    g1_ref[...] = g1_in[...].astype(F32)
    g2_ref[...] = g2_in[...].astype(F32)


def shards(tokens, w_first, w_second, cotangent):
    hbm = pl.BlockSpec(memory_space=pl.ANY)
    parts = pl.pallas_call(
        kernel,
        name="mlp",
        out_shape=(
            jax.ShapeDtypeStruct((192, TOK), BF16),
            jax.ShapeDtypeStruct((192, TOK), BF16),
            jax.ShapeDtypeStruct((B, 2 * B), BF16),
            jax.ShapeDtypeStruct((2 * B, B), BF16),
        ),
        in_specs=[hbm] * 4,
        out_specs=(hbm,) * 4,
        scratch_shapes=[
            pltpu.VMEM((D, HID), BF16),
            pltpu.VMEM((HID, D), BF16),
            pltpu.VMEM((TOK, D), BF16),
            pltpu.VMEM((TOK, D), BF16),
            pltpu.VMEM((D, TOK), BF16),
            pltpu.VMEM((TOK, HID), BF16),
            pltpu.VMEM((HID, TOK), BF16),
            pltpu.VMEM((TOK, HID), F32),
            pltpu.VMEM((TOK, HID), BF16),
            pltpu.VMEM((TOK, D), BF16),
            pltpu.VMEM((D, HID), BF16),
            pltpu.VMEM((HID, D), BF16),
            pltpu.VMEM((4, 2, B, B), BF16),
            pltpu.VMEM((4, 2, B, B), BF16),
            pltpu.VMEM((2, B, B), BF16),
            pltpu.VMEM((2, B, B), BF16),
            pltpu.VMEM((2, 2, B, B), BF16),
            pltpu.VMEM((2, 2, B, B), BF16),
            pltpu.VMEM((2, 4, RA, B), BF16),
            pltpu.VMEM((2, 2, 4, RA, B), BF16),
            pltpu.VMEM((2, 2, SPLIT_A[0], B), BF16),
            pltpu.VMEM((2, 2, RA, B), BF16),
            pltpu.VMEM((2, 4, RB, B), BF16),
            pltpu.VMEM((2, 2, 4, RB, B), BF16),
            pltpu.VMEM((2, 2, SPLIT_B[0], B), BF16),
            pltpu.VMEM((2, 2, RB, B), BF16),
            pltpu.VMEM((2, 192, HALF), BF16),
            pltpu.VMEM((2, 192, HALF), BF16),
            pltpu.VMEM((4, 2, B // 2, B), BF16),
            pltpu.VMEM((2, 192, TOK), BF16),
            pltpu.VMEM((2, 192, HALF), BF16),
            pltpu.SemaphoreType.DMA((2,)),
            pltpu.SemaphoreType.DMA((NSEM,)),
            pltpu.SemaphoreType.DMA((8,)),
        ],
        compiler_params=pltpu.CompilerParams(
            collective_id=0, has_side_effects=True, vmem_limit_bytes=60 * 1024 * 1024
        ),
        cost_estimate=pl.CostEstimate(flops=14_500_000_000, bytes_accessed=40_000_000, transcendentals=800_000),
    )(tokens.T, cotangent.T, w_first, w_second)
    steps = 2
    specs = [pl.BlockSpec((part.shape[0] // steps, part.shape[1]), lambda i: (i, 0)) for part in parts]
    outputs, input_grad, first_grad, second_grad = pl.pallas_call(
        widen,
        name="widen",
        grid=(steps,),
        out_shape=[
            jax.ShapeDtypeStruct(part.shape, dtype) for part, dtype in zip(parts, (BF16, BF16, F32, F32))
        ],
        in_specs=specs,
        out_specs=specs,
    )(*parts)
    return outputs.T, input_grad.T, first_grad, second_grad


def solution(mesh):
    finer = Mesh(mesh.devices.reshape(2, 4, 4, 2, 2), AXES)
    in_specs = (P(DP, MP), P(DP, MP), P(MP, DP), P(DP, MP))
    out_specs = (P(DP, MP), P(DP, MP), P(DP, MP), P(MP, DP))
    return jax.shard_map(
        shards, mesh=finer, in_specs=in_specs, out_specs=out_specs, check_vma=False
    )
```

```python
import jax
import jax.numpy as jnp
from jax import lax
from jax.experimental import pallas as pl
from jax.experimental.pallas import tpu as pltpu
from jax.sharding import Mesh
from jax.sharding import PartitionSpec as P

AXES = ("xh", "z", "y", "xl", "c")
DP = ("xh", "z")
MP = ("y", "xl", "c")
MESH = pl.DeviceIdType.MESH
F32 = jnp.float32
BF16 = jnp.bfloat16

D = 3072
B = 384
HID = 768
TOK = 512
HALF = 256
RA = 176
RB = HALF - RA
SPLIT_A = (96, 80)
SPLIT_B = (48, 32)
NSEM = 156

inv_root_two = 0.7071067811865476
inv_root_tau = 0.3989422804014327


def dot(a, b):
    return jnp.dot(a, b, preferred_element_type=F32)


def dot_nt(a, b):
    return lax.dot_general(a, b, (((1,), (1,)), ((), ())), preferred_element_type=F32)


def dot_tn(a, b):
    return lax.dot_general(a, b, (((0,), (0,)), ((), ())), preferred_element_type=F32)


def mult(value, of):
    return pl.multiple_of(value, of)


class Links:
    def __init__(self, send, recv, early):
        self.send, self.recv, self.early, self.count = send, recv, early, 0
        self.open, self.flushed = ([], []), False
        self.sems, self.shared = 0, {}

    def start(self, src, dst, peer, *share):
        i = self.count
        self.count += 1
        sem = self.shared.get(share, self.sems)
        if sem == self.sems:
            self.sems += 1
        if share:
            self.shared[share] = sem
        group = int(getattr(src, "ref", src) is self.early and not self.flushed)
        copy = pltpu.make_async_remote_copy(
            src_ref=src,
            dst_ref=dst,
            send_sem=self.send.at[group],
            recv_sem=self.recv.at[sem],
            device_id=peer,
            device_id_type=MESH,
        )
        copy.start()
        self.open[group].append(copy)
        return i, peer, sem

    def arrived(self, handle, where):
        i, peer, sem = handle
        pltpu.make_async_remote_copy(
            src_ref=where,
            dst_ref=where,
            send_sem=self.send.at[0],
            recv_sem=self.recv.at[sem],
            device_id=peer,
            device_id_type=MESH,
        ).wait_recv()

    def flush(self, group):
        for copy in self.open[group]:
            copy.wait_send()
        self.flushed = True


def kernel(
    tok_in, cot_in, w1_in, w2_in,
    out_ref, ing_ref, g1_ref, g2_ref,
    w1, w2, tok, cot, tok_t, act, act_t, slope, hg, oterm, p1, p2,
    rsw1, rsw2, rza1, rza2, rzb1, rzb2,
    ra1, ra2, ra3, ra4, rb1, rb2, rb3, rb4,
    swap_in, swap_out, stage, shards, results, send, recv, local,
):
    xh, z, y, xl, c = (lax.axis_index(a) for a in AXES)
    x = xh * 2 + xl
    xp, xm = lax.rem(x + 1, 4), lax.rem(x + 3, 4)
    ph, pll = xp // 2, lax.rem(xp, 2)
    mh, ml = xm // 2, lax.rem(xm, 2)
    yp, ym, y2 = lax.rem(y + 1, 4), lax.rem(y + 3, 4), lax.rem(y + 2, 4)
    zp, zm, z2 = lax.rem(z + 1, 4), lax.rem(z + 3, 4), lax.rem(z + 2, 4)
    oc = 1 - c
    XP, XM = {"xh": ph, "xl": pll}, {"xh": mh, "xl": ml}
    YP, YM, ZP, ZM, OC = {"y": yp}, {"y": ym}, {"z": zp}, {"z": zm}, {"c": oc}
    H = B // 2
    OWN, OTHER = 0, 1
    own_h, other_h = xh, 1 - xh
    links = Links(send, recv, tok)
    start, arrived = links.start, links.arrived

    loads = [
        pltpu.make_async_copy(ref, shards.at[k], local.at[4 + k]) for k, ref in enumerate((tok_in, cot_in))
    ]
    for load in loads:
        load.start()
    bar = pltpu.get_barrier_semaphore()
    for peer in (XP, XM, YP, YM, ZP, ZM, OC):
        pl.semaphore_signal(bar, inc=1, device_id=peer, device_id_type=MESH)
    pl.semaphore_wait(bar, 7)

    def rows_a(hv, lo=0, n=RA):
        return pl.ds(mult(hv * RA + lo, 16), n)

    def rows_b(hv, lo=0, n=RB):
        return pl.ds(mult(2 * RA + hv * RB + lo, 16), n)

    def cols(yv, lv):
        return pl.ds(mult((yv * 2 + lv) * B, 128), B)

    def line(yv):
        return pl.ds(mult(yv * 2 * B, 128), 2 * B)

    def loc1(ref, hv, zv, cv, lo=0, n=B):
        return ref.at[pl.ds(mult((hv * 4 + zv) * B + lo, 64), n), pl.ds(mult(cv * B, 128), B)]

    def loc2(ref, hv, zv, cv, lo=0, n=B):
        return ref.at[pl.ds(mult(cv * B + lo, 64), n), pl.ds(mult((hv * 4 + zv) * B, 128), B)]

    def half1(ref, hv, lo=0, n=B):
        return ref.at[pl.ds(lo, n), pl.ds(mult(hv * B, 128), B)]

    def half2(ref, hv, lo=0, n=B):
        return ref.at[pl.ds(mult(hv * B + lo, 64), n), :]

    class Weights:
        def __init__(self, k, shard, ref, loc, half, theirs):
            self.at = lambda b, zv, *part: loc(ref, (own_h, other_h)[b], zv, c, *part)
            self.theirs = theirs
            self.relayed = lambda hv, *part: loc(ref, hv, z, c, *part)
            self.swaps, self.z1, self.z2 = [], {}, {}
            self.k, self.shard, self.half = k, shard, half

        def swap(self, b, zv, src=None):
            block = self.at(b, zv)
            self.swaps.append(start(block if src is None else src, block, OC, "w", self.k))

        def exchange(self):
            self.x1 = tuple(
                start(self.half(self.shard, other_h, lo, H), stage.at[self.k, i], peer)
                for i, (lo, peer) in enumerate(((0, XP), (H, XM)))
            )

        def relay(self):
            arrived(self.x1[0], stage.at[self.k, 0])
            s0 = start(stage.at[self.k, 0], self.relayed(mh, 0, H), XP, "x", self.k)
            arrived(self.x1[1], stage.at[self.k, 1])
            s1 = start(stage.at[self.k, 1], self.relayed(ph, H, H), XM, "x", self.k)
            self.x2 = s0, s1

        def own(self):
            src, dst = self.half(self.shard, own_h), self.at(OWN, z)
            self.z1[OWN] = start(src, dst, ZP), start(src, dst, ZM)
            self.swap(OWN, z, src)
            self.copy = pltpu.make_async_copy(src, dst, local.at[self.k])
            self.copy.start()

        def partner(self):
            block = self.at(OTHER, z)
            arrived(self.x2[0], block)
            self.z1[OTHER] = start(block, block, ZP), start(block, block, ZM)
            self.swap(OTHER, z)

        def forward(self, b):
            p, m = self.z1[b]
            from_m, from_p = self.at(b, zm), self.at(b, zp)
            if b == OWN:
                arrived(p, from_m)
                self.z2[b] = start(from_m, from_m, ZP)
                arrived(m, from_p)
            else:
                arrived(m, from_p)
                self.z2[b] = start(from_p, from_p, ZM)
                arrived(p, from_m)
            self.swap(b, zm)
            self.swap(b, zp)

        def last(self, b):
            arrived(self.z2[b], self.at(b, z2))
            self.swap(b, z2)

        def whole(self):
            self.copy.wait()
            arrived(self.swaps[0], self.theirs)

    xs = {"o": (xh, xl), "m": (mh, ml), "p": (ph, pll), "t": (1 - xh, xl)}
    ys = {"o": y, "m": ym, "p": yp, "t": y2}
    PLUS = "om"

    def place_a(ref, i, j, lo=0, n=RA):
        (hv, lv), yv = xs[i], ys[j]
        return ref.at[rows_a(hv, lo, n), cols(yv, lv)]

    def place_b(ref, i, j, lo=0, n=RB):
        (hv, lv), yv = xs[j], ys[i]
        return ref.at[rows_b(hv, lo, n), cols(yv, lv)]

    ROUTES = {"a": (place_a, SPLIT_A, (XP, XM), (YP, YM)), "b": (place_b, SPLIT_B, (YP, YM), (XP, XM))}

    pick_row = lax.broadcasted_iota(jnp.int32, (192, B), 0)
    pick_col = lax.broadcasted_iota(jnp.int32, (192, B), 1)
    ours = (pick_col == pick_row + 192 * c).astype(BF16)
    theirs = (pick_col == pick_row + 192 * oc).astype(BF16)

    class GatherPart:
        def __init__(self, ref, route, k):
            self.route, self.k, self.key = route, k, ("g", k) if route == "a" else ()
            self.far_line = ref.at[pl.ds(0, 2 * RA), line(y2)]
            place, self.split, self.first, self.second = ROUTES[route]
            self.at = lambda *where: place(ref, *where)
            self.f2, self.s1, self.s2 = {}, {}, {}

        def both(self, i):
            block = self.at(i, "o")
            self.s1[i] = tuple(start(block, block, peer) for peer in self.second)

        def own_first(self):
            block = self.at("o", "o")
            self.f1 = tuple(start(block, block, peer) for peer in self.first)

        def near(self, i):
            n0, n1 = self.split
            p, m = self.first
            if i == "m":
                arrived(self.f1[0], self.at("m", "o"))
                block = self.at("m", "o", 0, n0)
                self.f2[0] = start(block, block, p, "f", self.route, self.k)
            else:
                arrived(self.f1[1], self.at("p", "o"))
                block = self.at("p", "o", n0, n1)
                self.f2[1] = start(block, block, m, "f", self.route, self.k)
            self.both(i)

        def far(self):
            arrived(self.f2[0], self.at("t", "o"))
            self.both("t")

        def forward(self, i):
            from_m, from_p = self.at(i, "m"), self.at(i, "p")
            if i in PLUS:
                arrived(self.s1[i][0], from_m)
                self.s2[i] = start(from_m, from_m, self.second[0], *self.key)
                arrived(self.s1[i][1], from_p)
            else:
                arrived(self.s1[i][1], from_p)
                self.s2[i] = start(from_p, from_p, self.second[1], *self.key)
                arrived(self.s1[i][0], from_m)

        def whole(self):
            if self.key:
                arrived(self.s2["o"], self.far_line)
            else:
                for i in "ompt":
                    arrived(self.s2[i], self.at(i, "t"))

    class Gather:
        def __init__(self, shard, ref, k):
            self.ref, self.shard, self.k = ref, shard, k
            self.a, self.b = GatherPart(ref, "a", k), GatherPart(ref, "b", k)

        def swap(self):
            src = self.shard.at[:, pl.ds(mult(oc * HALF, HALF), HALF)]
            self.swapped = start(src, swap_in.at[self.k], OC)

        def assemble(self):
            arrived(self.swapped, swap_in.at[self.k])
            loads[self.k].wait()
            mine = shards[self.k, :, pl.ds(mult(c * HALF, HALF), HALF)]
            block = (dot_tn(mine, ours) + dot_tn(swap_in[self.k], theirs)).astype(BF16)
            self.ref[rows_a(xh), cols(y, xl)] = block[:RA]
            self.ref[rows_b(xh), cols(y, xl)] = block[RA:]

        def whole(self):
            self.a.whole()
            self.b.whole()

        def flush(self):
            links.flush(1)

    def add_into(where, *parts):
        total = where[...].astype(F32)
        for part in parts:
            total = total + part.astype(F32)
        where[...] = total.astype(BF16)

    class SumPart:
        def __init__(self, ref, route, k, r1, r2, r3, r4):
            place, self.split, self.first, self.second = ROUTES[route]
            self.at = lambda *where: place(ref, *where)
            self.key = "s", route, k
            self.r1, self.r2, self.r3, self.r4 = r1.at[k], r2.at[k], r3.at[k], r4.at[k]
            self.s0, self.s1, self.s2, self.s4 = {}, {}, {}, {}

        def far(self, i):
            n = "ompt".index(i)
            peer = self.second[0] if i in PLUS else self.second[1]
            self.s1[i] = start(self.at(i, "t"), self.r1.at[n], peer)

        def early(self, i):
            n = "ompt".index(i)
            if i in PLUS:
                self.s0[i] = start(self.at(i, "m"), self.r2.at[1, n], self.second[1], *self.key, i)
            else:
                self.s0[i] = start(self.at(i, "p"), self.r2.at[0, n], self.second[0], *self.key, i)

        def near(self, i):
            n = "ompt".index(i)
            arrived(self.s1[i], self.r1.at[n])
            if i in PLUS:
                add_into(self.at(i, "p"), self.r1[n])
                p = start(self.at(i, "p"), self.r2.at[0, n], self.second[0], *self.key, i)
                self.s2[i] = p, self.s0[i]
            else:
                add_into(self.at(i, "m"), self.r1[n])
                m = start(self.at(i, "m"), self.r2.at[1, n], self.second[1], *self.key, i)
                self.s2[i] = self.s0[i], m

        def summed(self, i, wait=True):
            n = "ompt".index(i)
            if wait:
                arrived(self.s2[i][0], self.r2.at[:, n])
            return self.r2[0, n], self.r2[1, n]

        def first_far(self):
            add_into(self.at("t", "o"), *self.summed("t"))
            n0, n1 = self.split
            self.s3 = (
                start(self.at("t", "o", 0, n0), self.r3.at[0, pl.ds(0, n0)], self.first[0]),
                start(self.at("t", "o", n0, n1), self.r3.at[1, pl.ds(0, n1)], self.first[1]),
            )

        def first_near(self, i):
            n0, n1 = self.split
            if i == "p":
                arrived(self.s3[0], self.r3.at[0, pl.ds(0, n0)])
                add_into(self.at("p", "o", n0, n1), *(r[n0:] for r in self.summed("p")))
                add_into(self.at("p", "o", 0, n0), self.r3[0, :n0], *(r[:n0] for r in self.summed("p", False)))
                self.s4[0] = start(self.at("p", "o"), self.r4.at[0], self.first[0])
            else:
                arrived(self.s3[1], self.r3.at[1, pl.ds(0, n1)])
                add_into(self.at("m", "o", 0, n0), *(r[:n0] for r in self.summed("m")))
                add_into(self.at("m", "o", n0, n1), self.r3[1, :n1], *(r[n0:] for r in self.summed("m", False)))
                self.s4[1] = start(self.at("m", "o"), self.r4.at[1], self.first[1])

        def total(self):
            parts = self.summed("o")
            arrived(self.s4[0], self.r4.at[0])
            arrived(self.s4[1], self.r4.at[1])
            value = self.at("o", "o")[...].astype(F32)
            for part in (*parts, self.r4[0], self.r4[1]):
                value = value + part.astype(F32)
            return value.astype(BF16)

    class Plane:
        def __init__(self, ref, k, result):
            self.k, self.result = k, result
            self.a = SumPart(ref, "a", k, ra1, ra2, ra3, ra4)
            self.b = SumPart(ref, "b", k, rb1, rb2, rb3, rb4)

        def done(self):
            k = self.k
            total = jnp.concatenate([self.a.total(), self.b.total()], axis=0)
            mine = pl.ds(mult(c * HALF, HALF), HALF)
            swap_out[k] = dot_nt(theirs, total).astype(BF16)
            self.last = start(swap_out.at[k], self.result.at[:, mine], OC)
            results[k] = dot_nt(ours, total).astype(BF16)
            self.copy = pltpu.make_async_copy(results.at[k], self.result.at[:, mine], local.at[6 + k])
            self.copy.start()

        def whole(self):
            self.copy.wait()
            arrived(self.last, self.result.at[:, pl.ds(mult(oc * HALF, HALF), HALF)])

    class Grad:
        def __init__(self, k, ref, loc, rsw, rz1, rz2, result, half):
            self.at = lambda b, zv, *part: loc(ref, (own_h, other_h)[b], zv, c, *part)
            self.theirs = lambda b, zv: loc(ref, (own_h, other_h)[b], zv, oc)
            self.k, self.rsw, self.rz1, self.rz2, self.result, self.half = k, rsw, rz1, rz2, result, half
            self.swaps, self.s0, self.s1, self.s2 = {}, {}, {}, {}

        def swap(self, j, zv, b):
            self.swaps[j, b] = start(self.theirs(b, zv), self.rsw.at[j, b], OC)

        def swapped(self, j, zv, b):
            arrived(self.swaps[j, b], self.rsw.at[j, b])
            add_into(self.at(b, zv), self.rsw[j, b])

        def far(self, b):
            self.s1[b] = start(self.at(b, z2), self.rz1.at[b], ZP if b == OWN else ZM)

        def early(self, b):
            if b == OWN:
                self.swapped(2, zm, b)
                self.s0[b] = start(self.at(b, zm), self.rz2.at[1, b], ZM, "t", self.k, b)
            else:
                self.swapped(1, zp, b)
                self.s0[b] = start(self.at(b, zp), self.rz2.at[0, b], ZP, "t", self.k, b)

        def near(self, b):
            arrived(self.s1[b], self.rz1.at[b])
            j, zv = (1, zp) if b == OWN else (2, zm)
            arrived(self.swaps[j, b], self.rsw.at[j, b])
            add_into(self.at(b, zv), self.rsw[j, b], self.rz1[b])
            if b == OWN:
                self.s2[b] = start(self.at(b, zp), self.rz2.at[0, b], ZP, "t", self.k, b), self.s0[b]
            else:
                self.s2[b] = self.s0[b], start(self.at(b, zm), self.rz2.at[1, b], ZM, "t", self.k, b)

        def total(self, b):
            arrived(self.s2[b][0], self.rz2.at[:, b])
            arrived(self.swaps[3, b], self.rsw.at[3, b])
            add_into(self.at(b, z), self.rsw[3, b], self.rz2[0, b], self.rz2[1, b])
            if b == OWN:
                self.copy = pltpu.make_async_copy(
                    self.at(b, z), self.half(self.result, own_h), local.at[self.k]
                )
                self.copy.start()
            else:
                self.s3 = tuple(
                    start(self.at(b, z, lo, H), stage.at[self.k, i], peer)
                    for i, (lo, peer) in enumerate(((0, XP), (H, XM)))
                )

        def relay(self):
            arrived(self.s3[0], stage.at[self.k, 0])
            s0 = start(stage.at[self.k, 0], self.half(self.result, mh, 0, H), XP, "x", self.k)
            arrived(self.s3[1], stage.at[self.k, 1])
            s1 = start(stage.at[self.k, 1], self.half(self.result, ph, H, H), XM, "x", self.k)
            self.s4 = s0, s1

        def whole(self):
            self.copy.wait()
            arrived(self.s4[0], self.half(self.result, other_h))

    def transpose_tokens():
        @pl.loop(0, D // 256)
        def _(j):
            at = pl.ds(mult(j * 256, 256), 256)
            tok_t[at, :] = tok[:, at].T

    def hidden(j):
        at = pl.ds(j * 256, 256)
        for lo in range(0, TOK, 256):
            rows = pl.ds(lo, 256)
            pre = dot(tok[rows, :], w1[:, at])
            cdf = 0.5 * (1.0 + lax.erf(pre * inv_root_two))
            value = (pre * cdf).astype(BF16)
            act[rows, at] = value
            act_t[at, rows] = value.T
            slope[rows, at] = cdf + pre * jnp.exp(-0.5 * pre * pre) * inv_root_tau

    def output_terms(yv):
        oterm[:, line(yv)] = dot(act[...], w2[:, line(yv)]).astype(BF16)

    def second_terms(zv, b):
        at = pl.ds(mult(((own_h, other_h)[b] * 4 + zv) * B, 128), B)
        p2[:, at] = dot(act_t[...], cot[:, at]).astype(BF16)

    def hidden_grad(j):
        at = pl.ds(j * 256, 256)
        for lo in range(0, TOK, 256):
            rows = pl.ds(lo, 256)
            back = dot_nt(cot[rows, :], w2[at, :])
            hg[rows, at] = (back * slope[rows, at]).astype(BF16)

    def first_terms(zv, b):
        at = pl.ds(mult(((own_h, other_h)[b] * 4 + zv) * B, 128), B)
        p1[at, :] = dot(tok_t[at, :], hg[...]).astype(BF16)

    def input_terms(yv):
        tok[:, line(yv)] = dot_nt(hg[...], w1[line(yv), :]).astype(BF16)

    of_theirs = pl.ds(mult(oc * B, 128), B)
    wf = Weights(0, w1_in, w1, loc1, half1, w1.at[:, of_theirs])
    ws = Weights(1, w2_in, w2, loc2, half2, w2.at[of_theirs, :])
    gt = Gather(tok_in, tok, 0)
    gc = Gather(cot_in, cot, 1)
    po = Plane(oterm, 0, out_ref)
    pi = Plane(tok, 1, ing_ref)
    gs = Grad(2, p2, loc2, rsw2, rza2, rzb2, g2_ref, half2)
    gf = Grad(3, p1, loc1, rsw1, rza1, rzb1, g1_ref, half1)
    wf.exchange()
    gt.swap()
    gc.swap()
    wf.own()
    ws.own()
    gt.assemble()
    gt.b.own_first()
    gt.a.own_first()
    gc.assemble()
    gt.a.both("o")
    wf.relay()
    ws.exchange()
    gc.b.own_first()
    gc.a.both("o")
    gt.a.near("m")
    gt.a.near("p")
    wf.partner()
    wf.forward(OWN)
    ws.relay()
    gc.a.own_first()
    gt.a.forward("m")
    gt.b.near("m")
    gc.b.near("p")
    gt.a.far()
    gt.b.near("p")
    ws.partner()
    gt.a.forward("p")
    wf.forward(OTHER)
    gt.b.far()
    ws.forward(OWN)
    gt.b.both("o")
    gc.a.near("m")
    gc.a.near("p")
    gt.b.forward("m")
    gc.b.near("m")
    gt.a.forward("o")
    gt.a.forward("t")
    gt.b.forward("t")
    gt.b.forward("p")
    gt.b.forward("o")
    gc.a.far()
    wf.last(OWN)
    ws.forward(OTHER)
    gc.a.forward("m")
    gc.b.far()
    gc.b.both("o")
    wf.last(OTHER)
    gt.whole()
    gc.a.forward("p")
    gc.b.forward("m")
    gc.a.forward("o")
    transpose_tokens()
    gc.b.forward("t")
    wf.whole()
    hidden(0)
    gc.b.forward("p")
    gc.b.forward("o")
    gc.a.forward("t")
    hidden(2)
    ws.last(OWN)
    ws.last(OTHER)
    hidden(1)
    ws.whole()
    output_terms(y2)
    gt.flush()
    po.a.far("t")
    gc.whole()
    po.b.far("t")
    po.b.early("t")
    po.a.far("m")
    second_terms(z2, OTHER)
    gs.swap(0, z2, OTHER)
    second_terms(zp, OTHER)
    gs.swap(1, zp, OTHER)
    output_terms(ym)
    output_terms(yp)
    gs.swapped(0, z2, OTHER)
    gs.far(OTHER)
    po.a.early("m")
    po.a.early("t")
    po.b.early("m")
    po.b.far("m")
    po.a.far("p")
    po.b.early("p")
    po.a.early("p")
    po.b.far("p")
    po.a.far("o")
    po.b.near("t")
    gs.early(OTHER)
    hidden_grad(0)
    hidden_grad(1)
    hidden_grad(2)
    first_terms(z2, OTHER)
    gf.swap(0, z2, OTHER)
    po.b.near("m")
    first_terms(zp, OTHER)
    gf.swap(1, zp, OTHER)
    po.a.near("t")
    input_terms(y2)
    pi.b.far("t")
    pi.b.early("t")
    input_terms(yp)
    gf.swapped(0, z2, OTHER)
    pi.b.far("p")
    gf.far(OTHER)
    po.b.near("p")
    pi.a.far("t")
    pi.b.early("p")
    pi.a.early("t")
    second_terms(z2, OWN)
    gf.early(OTHER)
    output_terms(y)
    gs.swap(0, z2, OWN)
    po.b.far("o")
    input_terms(y)
    pi.b.far("o")
    po.b.first_far()
    second_terms(zm, OTHER)
    pi.b.near("t")
    second_terms(z, OWN)
    gs.swapped(0, z2, OWN)
    gs.swap(2, zm, OTHER)
    first_terms(zm, OTHER)
    po.a.first_far()
    first_terms(zm, OWN)
    po.a.near("m")
    po.a.near("p")
    pi.b.early("o")
    gf.swap(2, zm, OTHER)
    gs.swap(3, z, OWN)
    pi.b.near("p")
    gs.far(OWN)
    input_terms(ym)
    po.b.early("o")
    pi.b.far("m")
    gs.near(OTHER)
    pi.b.early("m")
    first_terms(z, OWN)
    gf.swap(2, zm, OWN)
    pi.b.near("o")
    first_terms(z2, OWN)
    gf.swap(3, z, OWN)
    pi.b.first_far()
    second_terms(zm, OWN)
    pi.a.far("m")
    po.b.near("o")
    gs.swap(2, zm, OWN)
    first_terms(z, OTHER)
    pi.a.far("o")
    gf.swap(0, z2, OWN)
    pi.a.near("t")
    pi.a.far("p")
    pi.a.early("m")
    first_terms(zp, OWN)
    pi.b.near("m")
    po.b.first_near("m")
    second_terms(zp, OWN)
    gf.near(OTHER)
    gf.swap(3, z, OTHER)
    second_terms(z, OTHER)
    po.b.first_near("p")
    pi.a.early("p")
    gf.swapped(0, z2, OWN)
    gf.swap(1, zp, OWN)
    gf.far(OWN)
    po.a.first_near("m")
    po.a.first_near("p")
    gs.early(OWN)
    gs.swap(3, z, OTHER)
    gs.swap(1, zp, OWN)
    pi.b.first_near("m")
    gf.early(OWN)
    gs.total(OTHER)
    pi.a.first_far()
    pi.a.near("p")
    pi.a.near("m")
    gs.relay()
    gs.near(OWN)
    gf.total(OTHER)
    pi.a.early("o")
    gf.near(OWN)
    pi.a.near("o")
    pi.a.first_near("p")
    pi.a.first_near("m")
    pi.b.first_near("p")
    po.a.early("o")
    po.a.near("o")
    gs.total(OWN)
    gf.relay()
    pi.done()
    po.done()
    gf.total(OWN)
    for part in (po, gs, gf, pi):
        part.whole()
    links.flush(0)


PARTS = 4


def widen(out_in, ing_in, g1_in, g2_in, out_ref, ing_ref, g1_ref, g2_ref, ov, iv, n1, n2, f1, f2, sems):
    loads, stores = [], []
    for i in range(PARTS):
        for k, (src, narrow, wide, dst) in enumerate(((g1_in, n1, f1, g1_ref), (g2_in, n2, f2, g2_ref))):
            rows = src.shape[0] // PARTS
            at = pl.ds(i * rows, rows)
            loads.append((pltpu.make_async_copy(src.at[at], narrow.at[at], sems.at[i, k, 0]), narrow, wide, at))
            stores.append(pltpu.make_async_copy(wide.at[at], dst.at[at], sems.at[i, k, 1]))
    for k, (src, held, dst) in enumerate(((out_in, ov, out_ref), (ing_in, iv, ing_ref))):
        loads.append((pltpu.make_async_copy(src, held, sems.at[0, k, 2]), held, None, None))
        stores.append(pltpu.make_async_copy(held, dst, sems.at[1, k, 2]))
    for copy, *_ in loads:
        copy.start()
    for (load, narrow, wide, at), store in zip(loads, stores):
        load.wait()
        if wide is not None:
            wide[at, :] = narrow[at, :].astype(F32)
        store.start()
    for copy in stores:
        copy.wait()


def shards(tokens, w_first, w_second, cotangent):
    hbm = pl.BlockSpec(memory_space=pl.ANY)
    parts = pl.pallas_call(
        kernel,
        name="mlp",
        out_shape=(
            jax.ShapeDtypeStruct((192, TOK), BF16),
            jax.ShapeDtypeStruct((192, TOK), BF16),
            jax.ShapeDtypeStruct((B, 2 * B), BF16),
            jax.ShapeDtypeStruct((2 * B, B), BF16),
        ),
        in_specs=[hbm] * 4,
        out_specs=(hbm,) * 4,
        scratch_shapes=[
            pltpu.VMEM((D, HID), BF16),
            pltpu.VMEM((HID, D), BF16),
            pltpu.VMEM((TOK, D), BF16),
            pltpu.VMEM((TOK, D), BF16),
            pltpu.VMEM((D, TOK), BF16),
            pltpu.VMEM((TOK, HID), BF16),
            pltpu.VMEM((HID, TOK), BF16),
            pltpu.VMEM((TOK, HID), F32),
            pltpu.VMEM((TOK, HID), BF16),
            pltpu.VMEM((TOK, D), BF16),
            pltpu.VMEM((D, HID), BF16),
            pltpu.VMEM((HID, D), BF16),
            pltpu.VMEM((4, 2, B, B), BF16),
            pltpu.VMEM((4, 2, B, B), BF16),
            pltpu.VMEM((2, B, B), BF16),
            pltpu.VMEM((2, B, B), BF16),
            pltpu.VMEM((2, 2, B, B), BF16),
            pltpu.VMEM((2, 2, B, B), BF16),
            pltpu.VMEM((2, 4, RA, B), BF16),
            pltpu.VMEM((2, 2, 4, RA, B), BF16),
            pltpu.VMEM((2, 2, SPLIT_A[0], B), BF16),
            pltpu.VMEM((2, 2, RA, B), BF16),
            pltpu.VMEM((2, 4, RB, B), BF16),
            pltpu.VMEM((2, 2, 4, RB, B), BF16),
            pltpu.VMEM((2, 2, SPLIT_B[0], B), BF16),
            pltpu.VMEM((2, 2, RB, B), BF16),
            pltpu.VMEM((2, 192, HALF), BF16),
            pltpu.VMEM((2, 192, HALF), BF16),
            pltpu.VMEM((4, 2, B // 2, B), BF16),
            pltpu.VMEM((2, 192, TOK), BF16),
            pltpu.VMEM((2, 192, HALF), BF16),
            pltpu.SemaphoreType.DMA((2,)),
            pltpu.SemaphoreType.DMA((NSEM,)),
            pltpu.SemaphoreType.DMA((8,)),
        ],
        compiler_params=pltpu.CompilerParams(
            collective_id=0, has_side_effects=True, vmem_limit_bytes=60 * 1024 * 1024
        ),
        cost_estimate=pl.CostEstimate(flops=14_500_000_000, bytes_accessed=40_000_000, transcendentals=800_000),
    )(tokens.T, cotangent.T, w_first, w_second)
    outputs, input_grad, first_grad, second_grad = pl.pallas_call(
        widen,
        name="widen",
        out_shape=[
            jax.ShapeDtypeStruct(part.shape, dtype) for part, dtype in zip(parts, (BF16, BF16, F32, F32))
        ],
        in_specs=[hbm] * 4,
        out_specs=[hbm] * 4,
        scratch_shapes=[
            *(pltpu.VMEM(part.shape, BF16) for part in parts),
            *(pltpu.VMEM(part.shape, F32) for part in parts[2:]),
            pltpu.SemaphoreType.DMA((PARTS, 2, 3)),
        ],
    )(*parts)
    return outputs.T, input_grad.T, first_grad, second_grad


def solution(mesh):
    finer = Mesh(mesh.devices.reshape(2, 4, 4, 2, 2), AXES)
    in_specs = (P(DP, MP), P(DP, MP), P(MP, DP), P(DP, MP))
    out_specs = (P(DP, MP), P(DP, MP), P(DP, MP), P(MP, DP))
    return jax.shard_map(
        shards, mesh=finer, in_specs=in_specs, out_specs=out_specs, check_vma=False
    )
```
